256 devices in a mesh: seq: 64 (over z, x, core), tp: 4 (over y).
Axes of the slice: x: 4, y: 4, z: 8, core: 2. Of those that a mesh axis runs over, the one named last changes fastest.
Arguments:
- tokens: bfloat16 [4, 16, 5120], P(None, None, 'seq'), may hold values from -32 to 32
- attn_gain: bfloat16 [5120], P('seq'), may hold values from 0.099609375 to 1.8984375
- w_query: bfloat16 [5120, 4096], P('seq', 'tp'), may hold values from -0.078125 to 0.078125
- w_key: bfloat16 [5120, 1024], P('seq', 'tp'), may hold values from -0.078125 to 0.078125
- w_value: bfloat16 [5120, 1024], P('seq', 'tp'), may hold values from -0.078125 to 0.078125
- w_out: bfloat16 [4096, 5120], P('tp', 'seq'), may hold values from -0.09375 to 0.09375
- ffn_gain: bfloat16 [5120], replicated, may hold values from 0.099609375 to 1.8984375
- w_gate: bfloat16 [5120, 32768], P(None, ('seq', 'tp')), may hold values from -0.078125 to 0.078125
- w_up: bfloat16 [5120, 32768], P(None, ('seq', 'tp')), may hold values from -0.078125 to 0.078125
- w_down: bfloat16 [32768, 5120], P(('seq', 'tp')), may hold values from -0.125 to 0.125
- key_cache: bfloat16 [16, 8192, 8, 128], P(None, 'seq', 'tp'), may hold values from -96 to 96
- value_cache: bfloat16 [16, 8192, 8, 128], P(None, 'seq', 'tp'), may hold values from -48 to 48
- lengths: int32 [16], replicated, may hold values from 1 to 8188, as said below
Outputs:
- hidden_out: bfloat16 [4, 16, 5120], P(None, None, 'seq')
- keys_out: bfloat16 [16, 8192, 8, 128], P(None, 'seq', 'tp')
- values_out: bfloat16 [16, 8192, 8, 128], P(None, 'seq', 'tp')
The draws below stay inside these ranges and needn't reach their ends.
Inputs may be any that keep to these rules, and one draw needn't show every extreme that they name: `lengths`: some request's length is exactly 8188.
All inputs are finite; a program needn't handle non-finite values.
Results may differ from the reference program's by a relative error of at most 0.012.
The reference program's roundings to bfloat16 on the way count: a program that leaves them out, or rounds other values in their place, can miss the bound.
Values may be sent and summed in bfloat16 or wider, within the bound.
A program may use at most 128 MiB of HBM per device.

```python
import math
import jax
import jax.numpy as jnp
from jax import lax

D = 5120
HEADS = 32
KVH = 8
HD = 128
FF = 32768
REQ = 16
STEPS = 4
SEQ_LEN = 8192


def draw_tokens(key, part):
    ramp = jnp.arange(D, dtype=jnp.float32) / D
    rise = jnp.exp(ramp * jnp.log(4.0))
    norm = jnp.sqrt(jnp.mean(rise * rise))
    base = jnp.clip(jax.random.normal(key, (STEPS, REQ, D), jnp.float32), -6.0, 6.0)
    values = base * (rise / norm)[None, None, :]
    return jnp.clip(values, -32.0, 32.0).astype(jnp.bfloat16)


def draw_lengths(key, part):
    longest = SEQ_LEN - STEPS
    drawn = jax.random.randint(jax.random.fold_in(key, 101), (REQ,), 1, longest + 1)
    chosen = jax.random.randint(jax.random.fold_in(key, 103), (), 0, REQ)
    return jnp.where(jnp.arange(REQ) == chosen, longest, drawn).astype(jnp.int32)


def stale_slots(key):
    lengths = draw_lengths(key, 0)
    places = jnp.arange(SEQ_LEN, dtype=jnp.int32)[None, :]
    return (places >= lengths[:, None]) & (places < lengths[:, None] + STEPS)


def stale_entries(key, low, high):
    magnitude = jax.random.uniform(jax.random.fold_in(key, 1), (REQ, SEQ_LEN, KVH, HD), jnp.float32, low, high)
    upward = jax.random.bernoulli(jax.random.fold_in(key, 2), 0.5, (REQ, SEQ_LEN, KVH, HD))
    return jnp.where(upward, magnitude, -magnitude)


def draw_key_cache(key, part):
    base = jax.random.normal(jax.random.fold_in(key, 201), (REQ, SEQ_LEN, KVH, HD), jnp.float32)
    scale = 2.5
    fresh = jnp.clip(base * scale, -96.0, 96.0)
    stale = stale_entries(jax.random.fold_in(key, 211), 48.0, 96.0)
    chosen = stale_slots(key)[:, :, None, None]
    return jnp.where(chosen, stale, fresh).astype(jnp.bfloat16)


def draw_value_cache(key, part):
    fresh = jnp.clip(jax.random.normal(jax.random.fold_in(key, 301), (REQ, SEQ_LEN, KVH, HD), jnp.float32), -6.0, 6.0)
    stale = stale_entries(jax.random.fold_in(key, 311), 24.0, 48.0)
    chosen = stale_slots(key)[:, :, None, None]
    return jnp.where(chosen, stale, fresh).astype(jnp.bfloat16)


def with_spikes(values, key, source, target, shards_of, factor):
    owner, partner = [(jnp.arange(values.shape[dim]) // (values.shape[dim] // shards_of)).reshape([-1 if axis == dim else 1 for axis in range(values.ndim)]) for dim in (source, target)]
    chosen = jax.random.permutation(key, shards_of)[partner]
    strong = (owner == chosen) | (owner == (partner + shards_of // 2) % shards_of)
    return jnp.where(strong, factor * values, values)


def block_levels(rng, dims, cuts, smallest, largest):
    def one(dim, blocks):
        steps = jax.random.uniform(jax.random.fold_in(jax.random.fold_in(rng, 6), dim), (blocks,), jnp.float32, smallest / len(cuts), largest / len(cuts))
        return jnp.repeat(jnp.exp(steps), dims[dim] // blocks).reshape((-1,) + (1,) * (len(dims) - dim - 1))

    gain = one(*cuts[0])
    for cut in cuts[1:]:
        gain = gain * one(*cut)
    return gain


def bell_draw(rng, shape, width, bound, split=(), held_as=jnp.bfloat16):
    array = width * jax.random.normal(rng, shape, jnp.float32)
    if split:
        array = array * block_levels(rng, shape, split, -0.22, 0.18)
    return jnp.clip(array, -bound, bound).astype(held_as)


def gaussian_with(own_key, extent, spread, bound, pieces, heavy, kind=jnp.bfloat16):
    array = spread * jax.random.normal(own_key, extent, jnp.float32)
    if pieces:
        array = array * block_levels(own_key, extent, pieces, -0.22, 0.18)
    return jnp.clip(with_spikes(array, jax.random.fold_in(own_key, 3), *heavy), -bound, bound).astype(kind)


def setup_inputs(seed: int = 0) -> dict:
    seeds = jax.random.split(jax.random.key(seed), 14)
    return {
        "tokens": draw_tokens(jax.random.fold_in(seeds[13], 71), 0),
        "attn_gain": jnp.clip(1.0 + 0.18 * jax.random.normal(seeds[1], (D,), jnp.float32), 0.099609375, 1.8984375).astype(jnp.bfloat16),
        "w_query": bell_draw(seeds[2], (D, HEADS * HD), D ** -0.5, 0.078125, ((0, 64), (1, 4))),
        "w_key": bell_draw(seeds[3], (D, KVH * HD), D ** -0.5, 0.078125, ((0, 64), (1, 4))),
        "w_value": bell_draw(seeds[4], (D, KVH * HD), D ** -0.5, 0.078125, ((0, 64), (1, 4))),
        "w_out": bell_draw(seeds[5], (HEADS * HD, D), (HEADS * HD) ** -0.5, 0.09375, ((0, 4), (1, 64))),
        "ffn_gain": jnp.clip(1.0 + 0.18 * jax.random.normal(seeds[6], (D,), jnp.float32), 0.099609375, 1.8984375).astype(jnp.bfloat16),
        "w_gate": bell_draw(seeds[7], (D, FF), D ** -0.5, 0.078125, ((1, 256),)),
        "w_up": bell_draw(seeds[8], (D, FF), D ** -0.5, 0.078125, ((1, 256),)),
        "w_down": gaussian_with(seeds[9], (FF, D), FF ** -0.5, 0.125, ((0, 256),), (0, 1, 256, 6.0)),
        "key_cache": draw_key_cache(jax.random.fold_in(seeds[13], 71), 0),
        "value_cache": draw_value_cache(jax.random.fold_in(seeds[13], 71), 0),
        "lengths": draw_lengths(jax.random.fold_in(seeds[13], 71), 0),
    }


def rotate(vectors, position):
    half = vectors.shape[-1] // 2
    freqs = jnp.exp(jnp.arange(half, dtype=jnp.float32) * (-2.0 * math.log(100000000.0) / vectors.shape[-1]))
    angles = position.astype(jnp.float32)[:, None] * freqs[None, :]
    cosine = jnp.cos(angles)[:, None, :]
    sine = jnp.sin(angles)[:, None, :]
    first = vectors[..., :half]
    second = vectors[..., half:]
    return jnp.concatenate([first * cosine - second * sine, second * cosine + first * sine], axis=-1)

def one_request(packed):
    query, keys, values, position = packed
    grouped = query.astype(jnp.float32).reshape(KVH, HEADS // KVH, HD)
    scores = jnp.einsum('gjd,pgd->gjp', grouped, keys.astype(jnp.float32)) * HD ** (-0.5)
    live = (jnp.arange(SEQ_LEN) <= position)[None, None, :]
    masked = jnp.where(live, scores, -1e+30)
    top = lax.optimization_barrier(jnp.max(masked, axis=-1))
    expo = jnp.where(live, jnp.exp(masked - top[..., None]), 0.0)
    denom = lax.optimization_barrier(jnp.sum(expo, axis=-1))
    weights = expo.astype(jnp.bfloat16)
    summed = jnp.einsum('gjp,pgd->gjd', weights.astype(jnp.float32), values.astype(jnp.float32))
    return (summed / denom[..., None]).reshape(HEADS, HD).astype(jnp.bfloat16)

def reference(tokens, attn_gain, w_query, w_key, w_value, w_out, ffn_gain, w_gate, w_up, w_down, key_cache, value_cache, lengths):
    req_index = jnp.arange(REQ)
    results = []
    for step in range(STEPS):
        residual = tokens[step].astype(jnp.float32)
        scale_in = lax.rsqrt(lax.optimization_barrier(jnp.mean(residual * residual, axis=1, keepdims=True)) + 1e-05)
        normed = (residual * attn_gain.astype(jnp.float32)).astype(jnp.bfloat16)
        query = jnp.dot(normed, w_query, preferred_element_type=jnp.float32) * scale_in
        key_new = jnp.dot(normed, w_key, preferred_element_type=jnp.float32) * scale_in
        value_new = jnp.dot(normed, w_value, preferred_element_type=jnp.float32) * scale_in
        position = (lengths + step).astype(jnp.int32)
        query = rotate(query.reshape(REQ, HEADS, HD), position).astype(jnp.bfloat16)
        key_new = rotate(key_new.reshape(REQ, KVH, HD), position).astype(jnp.bfloat16)
        value_new = value_new.reshape(REQ, KVH, HD).astype(jnp.bfloat16)
        key_cache = key_cache.at[req_index, position].set(key_new)
        value_cache = value_cache.at[req_index, position].set(value_new)
        attended = lax.map(one_request, (query, key_cache, value_cache, position))
        mixed = residual + jnp.dot(attended.reshape(REQ, HEADS * HD), w_out, preferred_element_type=jnp.float32)
        scale_mid = lax.rsqrt(lax.optimization_barrier(jnp.mean(mixed * mixed, axis=1, keepdims=True)) + 1e-05)
        ffn_in = (mixed * ffn_gain.astype(jnp.float32)).astype(jnp.bfloat16)
        gate_raw = jnp.dot(ffn_in, w_gate, preferred_element_type=jnp.float32) * scale_mid
        up_raw = jnp.dot(ffn_in, w_up, preferred_element_type=jnp.float32) * scale_mid
        hidden = (jax.nn.silu(gate_raw) * up_raw).astype(jnp.bfloat16)
        output = mixed + jnp.dot(hidden, w_down, preferred_element_type=jnp.float32)
        results.append(output.astype(jnp.bfloat16))
    return (jnp.stack(results), key_cache, value_cache)
```

```python
import math

import jax
import jax.numpy as jnp
from jax import lax
from jax.sharding import PartitionSpec as P

D = 5120
STEPS = 4
REQ = 16
ROWS = STEPS * REQ


def rotate(vectors, position):
    half = vectors.shape[-1] // 2
    freqs = jnp.exp(
        jnp.arange(half, dtype=jnp.float32) * (-2.0 * math.log(100000000.0) / vectors.shape[-1])
    )
    angles = position.astype(jnp.float32)[:, None] * freqs[None, :]
    cosine = jnp.cos(angles)[:, None, :]
    sine = jnp.sin(angles)[:, None, :]
    first = vectors[..., :half]
    second = vectors[..., half:]
    return jnp.concatenate(
        [first * cosine - second * sine, second * cosine + first * sine], axis=-1
    )


def per_device(
    tokens,
    attn_gain,
    w_query,
    w_key,
    w_value,
    w_out,
    ffn_gain,
    w_gate,
    w_up,
    w_down,
    key_cache,
    value_cache,
    lengths,
):
    span = key_cache.shape[1]
    kv_local = key_cache.shape[2]
    head_dim = key_cache.shape[3]
    width = tokens.shape[2]
    heads_local = w_query.shape[1] // head_dim
    group = heads_local // kv_local
    seq_index = lax.axis_index("seq")
    residual = tokens.reshape(ROWS, width).astype(jnp.float32)
    squares = jnp.sum(residual * residual, axis=1)
    normed = (residual * attn_gain.astype(jnp.float32)).astype(jnp.bfloat16)
    weights_in = jnp.concatenate([w_query, w_key, w_value], axis=1)
    part = jnp.dot(normed, weights_in, preferred_element_type=jnp.float32)
    part = jnp.concatenate([part, jnp.broadcast_to(squares[:, None], (ROWS, 128))], axis=1)
    total = lax.psum(part, "seq")
    scale_in = lax.rsqrt(total[:, -1:] / D + 1e-05)
    total = total[:, :-128] * scale_in
    qw, kw = w_query.shape[1], w_key.shape[1]
    position = (lengths[None, :] + jnp.arange(STEPS)[:, None]).reshape(ROWS)
    turned = rotate(
        total[:, : qw + kw].reshape(ROWS, heads_local + kv_local, head_dim), position
    ).astype(jnp.bfloat16)
    query = turned[:, :heads_local]
    key_new = turned[:, heads_local:].reshape(STEPS, REQ, kv_local, head_dim)
    value_new = total[:, qw + kw :].reshape(STEPS, REQ, kv_local, head_dim).astype(jnp.bfloat16)
    slot_pos = seq_index * span + jnp.arange(span)
    for step in range(STEPS):
        hit = (slot_pos[None, :] == (lengths + step)[:, None])[:, :, None, None]
        key_cache = jnp.where(hit, key_new[step][:, None], key_cache)
        value_cache = jnp.where(hit, value_new[step][:, None], value_cache)
    grouped = query.reshape(STEPS, REQ, kv_local, group, head_dim)
    scores = jnp.einsum(
        "trgjd,rpgd->rgtjp", grouped, key_cache, preferred_element_type=jnp.float32
    ) * head_dim ** (-0.5)
    live = slot_pos[None, None, :] <= position.reshape(STEPS, REQ).T[:, :, None]
    live = live[:, None, :, None, :]
    masked = jnp.where(live, scores, -1e30)
    local_top = jnp.max(masked, axis=-1)
    expo = jnp.where(live, jnp.exp(masked - local_top[..., None]), 0.0)
    local_total = jnp.sum(expo, axis=-1)
    local_out = jnp.einsum(
        "rgtjp,rpgd->rgtjd",
        expo.astype(jnp.bfloat16),
        value_cache,
        preferred_element_type=jnp.float32,
    )
    global_top = lax.pmax(local_top, "seq")
    factor = jnp.exp(local_top - global_top)[..., None]
    packed = jnp.concatenate(
        [local_out * factor, jnp.broadcast_to(local_total[..., None] * factor, local_out.shape)],
        axis=-1,
    )
    summed = lax.psum(packed, "seq")
    attended = (summed[..., :head_dim] / summed[..., head_dim : head_dim + 1]).astype(jnp.bfloat16)
    attended = attended.transpose(2, 0, 1, 3, 4).reshape(ROWS, heads_local * head_dim)
    projected = jnp.dot(attended, w_out, preferred_element_type=jnp.float32)
    mixed = residual + lax.psum(projected, "tp")
    own_gain = lax.dynamic_slice_in_dim(ffn_gain, seq_index * width, width, 0).astype(jnp.float32)
    ffn_in = (mixed * own_gain).astype(jnp.bfloat16)
    total_mid = lax.psum(jnp.sum(mixed * mixed, axis=1), "seq")
    piece = lax.all_gather(ffn_in, "seq", axis=1, tiled=True)
    gate_raw = jnp.dot(piece, w_gate, preferred_element_type=jnp.float32)
    up_raw = jnp.dot(piece, w_up, preferred_element_type=jnp.float32)
    scale_mid = lax.rsqrt(total_mid / D + 1e-05)[:, None]
    hidden = (jax.nn.silu(gate_raw * scale_mid) * (up_raw * scale_mid)).astype(jnp.bfloat16)
    down = jnp.dot(hidden, w_down, preferred_element_type=jnp.float32)
    down = lax.psum_scatter(down, "tp", scatter_dimension=0, tiled=True)
    down = lax.psum_scatter(down, "seq", scatter_dimension=1, tiled=True)
    ffn_part = lax.all_gather(down, "tp", axis=0, tiled=True)
    hidden_out = (mixed + ffn_part).astype(jnp.bfloat16).reshape(STEPS, REQ, width)
    return (hidden_out, key_cache, value_cache)


def solution(mesh):
    placed = (
        P(None, None, "seq"),
        P("seq"),
        P("seq", "tp"),
        P("seq", "tp"),
        P("seq", "tp"),
        P("tp", "seq"),
        P(),
        P(None, ("seq", "tp")),
        P(None, ("seq", "tp")),
        P(("seq", "tp"), None),
        P(None, "seq", "tp", None),
        P(None, "seq", "tp", None),
        P(),
    )
    return jax.shard_map(
        per_device,
        mesh=mesh,
        in_specs=placed,
        out_specs=(P(None, None, "seq"), P(None, "seq", "tp", None), P(None, "seq", "tp", None)),
        check_vma=False,
    )
```

```python
import functools
import math

import jax
import jax.numpy as jnp
from jax import lax
from jax.experimental import pallas as pl
from jax.experimental.pallas import tpu as pltpu
from jax.sharding import PartitionSpec as P

D = 5120
STEPS = 4
REQ = 16
ROWS = STEPS * REQ
SEQ = 64
TP = 4
WIDTH = D // SEQ
HD = 128
QH = 8
KH = 2
SPAN = 128
FFL = 128
LANES = 128
F32 = jnp.float32
BF16 = jnp.bfloat16
MESH = pl.DeviceIdType.MESH
NEG = -1e30


def split3(v):
    hi = v.astype(BF16).astype(F32)
    rest = v - hi
    mid = rest.astype(BF16).astype(F32)
    lo = rest - mid
    return hi, mid, lo


def kernel(
    tokens_ref,
    aux_ref,
    lengths_ref,
    wq_hbm,
    wk_hbm,
    wv_hbm,
    wo_hbm,
    wg_hbm,
    wu_hbm,
    wd_hbm,
    kc_hbm,
    vc_hbm,
    hid_ref,
    ko_hbm,
    vo_hbm,
    wqkv,
    wo,
    wgu,
    wd,
    kbuf,
    vbuf,
    xbuf,
    tmp,
    asrc,
    adst,
    bsrc,
    ball,
    csrc,
    cdst,
    dsrc,
    dall,
    ebuf,
    fall,
    gsrc,
    gdst,
    hsrc,
    hdst,
    ibuf,
    lsem,
    ssem,
    rsem,
):
    me = lax.axis_index("seq")
    mt = lax.axis_index("tp")

    barrier = pltpu.get_barrier_semaphore()

    @pl.loop(1, SEQ)
    def _(k):
        pl.semaphore_signal(
            barrier, inc=1, device_id=(lax.rem(me + k, SEQ), mt), device_id_type=MESH
        )

    @pl.loop(1, TP)
    def _(k):
        pl.semaphore_signal(
            barrier, inc=1, device_id=(me, lax.rem(mt + k, TP)), device_id_type=MESH
        )

    qw, kw = QH * HD, KH * HD
    loads = [
        (wq_hbm, wqkv.at[:, 0:qw]),
        (wk_hbm, wqkv.at[:, qw : qw + kw]),
        (wv_hbm, wqkv.at[:, qw + kw : qw + 2 * kw]),
        (kc_hbm, kbuf),
        (vc_hbm, vbuf),
        (wo_hbm, wo),
        (wg_hbm, wgu.at[:, 0:WIDTH, 0:FFL]),
        (wu_hbm, wgu.at[:, 0:WIDTH, FFL : 2 * FFL]),
        (wd_hbm, wd),
    ]
    copies = [pltpu.make_async_copy(s, d, lsem.at[i]) for i, (s, d) in enumerate(loads)]
    for c in copies:
        c.start()

    def seq_send(phase, source, target):
        @pl.loop(1, SEQ)
        def _(k):
            p = lax.rem(me + k, SEQ)
            pltpu.make_async_remote_copy(
                src_ref=source(p),
                dst_ref=target,
                send_sem=ssem.at[phase],
                recv_sem=rsem.at[phase],
                device_id=(p, mt),
                device_id_type=MESH,
            ).start()

    def tp_send(phase, source, target):
        @pl.loop(1, TP)
        def _(k):
            p = lax.rem(mt + k, TP)
            pltpu.make_async_remote_copy(
                src_ref=source(p),
                dst_ref=target,
                send_sem=ssem.at[phase],
                recv_sem=rsem.at[phase],
                device_id=(me, p),
                device_id_type=MESH,
            ).start()

    def arrived(phase, blocks):
        pltpu.make_async_copy(blocks, blocks, rsem.at[phase]).wait()

    def sent(phase, blocks):
        pltpu.make_async_copy(blocks, blocks, ssem.at[phase]).wait()

    xbuf[...] = jnp.zeros_like(xbuf)
    xbuf[:, 0:WIDTH] = tokens_ref[...].astype(F32).reshape(ROWS, WIDTH)
    x = xbuf[...]
    squares = jnp.sum(x * x, axis=1, keepdims=True)
    normed = (x * aux_ref[2:3, :]).astype(BF16)[:, 0:WIDTH]
    for piece, part in enumerate(split3(squares)):
        tmp[pl.ds(12 + piece, ROWS, stride=16), :] = jnp.broadcast_to(part, (ROWS, LANES))
    tmp[pl.ds(15, ROWS, stride=16), :] = jnp.zeros((ROWS, LANES), F32)
    for c in copies[0:3]:
        c.wait()
    for j in range(0, 12, 2):
        got = jnp.dot(normed, wqkv[:, j * HD : (j + 2) * HD], preferred_element_type=F32)
        tmp[pl.ds(j, ROWS, stride=16), :] = got[:, 0:HD]
        tmp[pl.ds(j + 1, ROWS, stride=16), :] = got[:, HD : 2 * HD]
    asrc[...] = tmp[...].reshape(ROWS, 16, LANES).astype(BF16)
    pl.semaphore_wait(barrier, SEQ - 1 + TP - 1)
    seq_send(0, lambda p: asrc.at[p], adst.at[me])
    adst[me] = asrc[me]
    wgu[:, WIDTH:LANES, :] = jnp.zeros((SEQ, LANES - WIDTH, 2 * FFL), BF16)
    hsrc[...] = jnp.zeros_like(hsrc)
    arrived(0, adst.at[0 : SEQ - 1])
    total = jnp.sum(adst[...].astype(F32), axis=0)
    scale_in = lax.rsqrt((total[12:13] + total[13:14] + total[14:15]) / D + 1e-05)
    scaled = total * scale_in
    turned = scaled * aux_ref[0:1, :] + pltpu.roll(scaled, HD // 2, 1) * aux_ref[1:2, :]
    sub = lax.broadcasted_iota(jnp.int32, (16, LANES), 0)
    row = jnp.where(sub < QH + KH, turned, jnp.where(sub < QH + 2 * KH, scaled, 0.0)).astype(BF16)
    bsrc[...] = row
    ball[me] = row
    seq_send(1, lambda p: bsrc, ball.at[me])

    first = me * SPAN
    r_i = lax.broadcasted_iota(jnp.int32, (2 * SPAN, ROWS), 0)
    c_i = lax.broadcasted_iota(jnp.int32, (2 * SPAN, ROWS), 1)
    where_new = r_i // 2 - c_i // 16
    pick_k = jnp.where(c_i % 16 == QH + r_i % 2, where_new, -100000)
    pick_v = jnp.where(c_i % 16 == QH + KH + r_i % 2, where_new, -100000)
    slot_i = lax.broadcasted_iota(jnp.int32, (2 * SPAN, HD), 0) // 2
    q_i = lax.broadcasted_iota(jnp.int32, (STEPS * QH, 2 * SPAN), 0)
    p_i = lax.broadcasted_iota(jnp.int32, (STEPS * QH, 2 * SPAN), 1)
    reach = jnp.where((q_i % QH) // (QH // KH) == p_i % 2, p_i // 2 - q_i // QH, 1 << 20)
    lane = lax.broadcasted_iota(jnp.int32, (STEPS * QH, LANES), 1)
    for c in copies[3:5]:
        c.wait()
    arrived(1, ball.at[0 : SEQ - 1])

    @pl.loop(0, REQ)
    def _(r):
        length = lengths_ref[r] - first
        news = [ball[t * REQ + r] for t in range(STEPS)]
        block = jnp.concatenate(news, axis=0)
        query = jnp.concatenate([n.astype(F32)[0:QH] for n in news], axis=0).astype(BF16)
        hot_k = jnp.where(pick_k == length, 1.0, 0.0).astype(BF16)
        hot_v = jnp.where(pick_v == length, 1.0, 0.0).astype(BF16)
        fresh_k = jnp.dot(hot_k, block, preferred_element_type=F32)
        fresh_v = jnp.dot(hot_v, block, preferred_element_type=F32)
        written = (slot_i >= length) & (slot_i < length + STEPS)
        keys = jnp.where(written, fresh_k, kbuf[r].astype(F32)).astype(BF16)
        values = jnp.where(written, fresh_v, vbuf[r].astype(F32)).astype(BF16)
        kbuf[r] = keys
        vbuf[r] = values
        scores = lax.dot_general(
            query, keys, (((1,), (1,)), ((), ())), preferred_element_type=F32
        ) * (HD ** (-0.5))
        live = reach <= length
        masked = jnp.where(live, scores, NEG)
        top = jnp.max(masked, axis=1, keepdims=True)
        expo = jnp.where(live, jnp.exp(masked - top), 0.0)
        denom = jnp.sum(expo, axis=1, keepdims=True)
        out = jnp.dot(expo.astype(BF16), values, preferred_element_type=F32)
        stats = jnp.zeros((STEPS * QH, LANES), F32)
        for i, piece in enumerate(split3(top) + split3(denom)):
            stats = jnp.where(lane == i, piece, stats)
        for t in range(STEPS):
            csrc[t * REQ + r] = jnp.concatenate(
                [out[t * QH : (t + 1) * QH], stats[t * QH : (t + 1) * QH]], axis=0
            ).astype(BF16)

    seq_send(2, lambda p: csrc.at[p], cdst.at[me])
    cdst[me] = csrc[me]
    outs = [
        pltpu.make_async_copy(kbuf, ko_hbm, lsem.at[9]),
        pltpu.make_async_copy(vbuf, vo_hbm, lsem.at[10]),
    ]
    for c in outs:
        c.start()
    arrived(2, cdst.at[0 : SEQ - 1])
    parts = cdst[...].astype(F32)
    stats = parts[:, QH : 2 * QH, :]
    lane8 = lax.broadcasted_iota(jnp.int32, (SEQ, QH, LANES), 2)
    tops = jnp.sum(jnp.where(lane8 < 3, stats, 0.0), axis=2, keepdims=True)
    dens = jnp.sum(jnp.where((lane8 >= 3) & (lane8 < 6), stats, 0.0), axis=2, keepdims=True)
    peak = jnp.max(tops, axis=0, keepdims=True)
    factor = jnp.exp(tops - peak)
    denom = jnp.sum(factor * dens, axis=0)
    attended = (jnp.sum(parts[:, 0:QH, :] * factor, axis=0) / denom).astype(BF16)
    dsrc[...] = attended
    dall[me] = attended
    seq_send(3, lambda p: dsrc, dall.at[me])
    copies[5].wait()
    arrived(3, dall.at[0 : SEQ - 1])
    tmp[0 : ROWS * QH, :] = dall[...].astype(F32).reshape(ROWS * QH, HD)
    projected = jnp.zeros((ROWS, WIDTH), F32)
    for h in range(0, QH, 2):
        left = jnp.concatenate(
            [tmp[pl.ds(h + i, ROWS, stride=QH), :].astype(BF16) for i in range(2)], axis=1
        )
        projected += lax.dot_general(
            left,
            wo[:, h * HD : (h + 2) * HD],
            (((1,), (1,)), ((), ())),
            preferred_element_type=F32,
        )
    ebuf[mt] = jnp.zeros((ROWS, LANES), F32)
    ebuf[mt, :, 0:WIDTH] = projected
    tp_send(4, lambda p: ebuf.at[mt], ebuf.at[mt])
    arrived(4, ebuf.at[0 : TP - 1])
    mixed = xbuf[...] + (ebuf[0] + ebuf[1] + ebuf[2] + ebuf[3])
    xbuf[...] = mixed
    ffn_in = mixed * aux_ref[3:4, :]
    lane64 = lax.broadcasted_iota(jnp.int32, (ROWS, LANES), 1)
    for i, piece in enumerate(split3(jnp.sum(mixed * mixed, axis=1, keepdims=True))):
        ffn_in = jnp.where(lane64 == WIDTH + i, piece, ffn_in)
    fall[me] = ffn_in.astype(BF16)
    seq_send(5, lambda p: fall.at[me], fall.at[me])
    for c in copies[6:9]:
        c.wait()
    arrived(5, fall.at[0 : SEQ - 1])
    both = jnp.zeros((ROWS, 2 * FFL), F32)
    seen = jnp.zeros((ROWS, LANES), F32)
    for i in range(0, SEQ, 2):
        one, two = fall[i], fall[i + 1]
        both += jnp.dot(
            jnp.concatenate([one, two], axis=1),
            wgu[i : i + 2].reshape(2 * LANES, 2 * FFL),
            preferred_element_type=F32,
        )
        seen += one.astype(F32) + two.astype(F32)
    total_mid = jnp.sum(
        jnp.where((lane64 >= WIDTH) & (lane64 < WIDTH + 3), seen, 0.0), axis=1, keepdims=True
    )
    scale_mid = lax.rsqrt(total_mid / D + 1e-05)
    gate = both[:, 0:FFL] * scale_mid
    up = both[:, FFL : 2 * FFL] * scale_mid
    hidden = ((gate / (1.0 + jnp.exp(-gate))) * up).astype(BF16)
    chunk = 512
    for c in range(0, D, chunk):
        down = jnp.dot(hidden, wd[:, c : c + chunk], preferred_element_type=F32).astype(BF16)
        gsrc[:, :, c : c + chunk] = down.reshape(TP, REQ, chunk)
    tp_send(6, lambda p: gsrc.at[p], gdst.at[mt])
    gdst[mt] = gsrc[mt]
    arrived(6, gdst.at[0 : TP - 1])
    for c in range(0, D, 5 * LANES):
        summed = jnp.sum(gdst[:, :, c : c + 5 * LANES].astype(F32), axis=0)
        for i in range(8):
            hsrc[c // WIDTH + i, :, 0:WIDTH] = summed[:, i * WIDTH : (i + 1) * WIDTH].astype(BF16)
    seq_send(7, lambda p: hsrc.at[p], hdst.at[me])
    hdst[me] = hsrc[me]
    arrived(7, hdst.at[0 : SEQ - 1])
    ibuf[mt] = jnp.sum(hdst[...].astype(F32), axis=0)
    tp_send(8, lambda p: ibuf.at[mt], ibuf.at[mt])
    arrived(8, ibuf.at[0 : TP - 1])
    final = xbuf[...] + ibuf[...].reshape(ROWS, LANES)
    hid_ref[...] = final.astype(BF16)[:, 0:WIDTH].reshape(STEPS, REQ, WIDTH)

    sent(0, adst.at[0 : SEQ - 1])
    sent(1, ball.at[0 : SEQ - 1])
    sent(2, cdst.at[0 : SEQ - 1])
    sent(3, dall.at[0 : SEQ - 1])
    sent(4, ebuf.at[0 : TP - 1])
    sent(5, fall.at[0 : SEQ - 1])
    sent(6, gdst.at[0 : TP - 1])
    sent(7, hdst.at[0 : SEQ - 1])
    sent(8, ibuf.at[0 : TP - 1])
    for c in outs:
        c.wait()


def per_device(
    tokens,
    attn_gain,
    w_query,
    w_key,
    w_value,
    w_out,
    ffn_gain,
    w_gate,
    w_up,
    w_down,
    key_cache,
    value_cache,
    lengths,
):
    me = lax.axis_index("seq")
    position = (lengths[lax.rem(me, REQ)] + me // REQ).astype(F32)
    freqs = jnp.exp(jnp.arange(HD // 2, dtype=F32) * (-2.0 * math.log(100000000.0) / HD))
    angles = position * freqs
    cosine, sine = jnp.cos(angles), jnp.sin(angles)
    own_gain = lax.dynamic_slice_in_dim(ffn_gain, me * WIDTH, WIDTH, 0).astype(F32)
    pad = (0, LANES - WIDTH)
    aux = jnp.stack(
        [
            jnp.concatenate([cosine, cosine]),
            jnp.concatenate([-sine, sine]),
            jnp.pad(attn_gain.astype(F32), pad),
            jnp.pad(own_gain, pad),
        ]
        + [jnp.zeros((LANES,), F32)] * 4
    )
    vm = pl.BlockSpec(memory_space=pltpu.VMEM)
    sm = pl.BlockSpec(memory_space=pltpu.SMEM)
    hb = pl.BlockSpec(memory_space=pl.ANY)
    cache = jax.ShapeDtypeStruct((REQ, 2 * SPAN, HD), BF16)
    hidden_out, keys, values = pl.pallas_call(
        kernel,
        out_shape=(jax.ShapeDtypeStruct((STEPS, REQ, WIDTH), BF16), cache, cache),
        in_specs=[vm, vm, sm] + [hb] * 9,
        out_specs=(vm, hb, hb),
        scratch_shapes=[
            pltpu.VMEM((WIDTH, (QH + 2 * KH) * HD), BF16),
            pltpu.VMEM((WIDTH, QH * HD), BF16),
            pltpu.VMEM((SEQ, LANES, 2 * FFL), BF16),
            pltpu.VMEM((FFL, D), BF16),
            pltpu.VMEM((REQ, 2 * SPAN, HD), BF16),
            pltpu.VMEM((REQ, 2 * SPAN, HD), BF16),
            pltpu.VMEM((ROWS, LANES), F32),
            pltpu.VMEM((ROWS * 16, LANES), F32),
            pltpu.VMEM((SEQ, 16, LANES), BF16),
            pltpu.VMEM((SEQ, 16, LANES), BF16),
            pltpu.VMEM((16, LANES), BF16),
            pltpu.VMEM((SEQ, 16, LANES), BF16),
            pltpu.VMEM((SEQ, 16, LANES), BF16),
            pltpu.VMEM((SEQ, 16, LANES), BF16),
            pltpu.VMEM((QH, HD), BF16),
            pltpu.VMEM((SEQ, QH, HD), BF16),
            pltpu.VMEM((TP, ROWS, LANES), F32),
            pltpu.VMEM((SEQ, ROWS, LANES), BF16),
            pltpu.VMEM((TP, REQ, D), BF16),
            pltpu.VMEM((TP, REQ, D), BF16),
            pltpu.VMEM((SEQ, REQ, LANES), BF16),
            pltpu.VMEM((SEQ, REQ, LANES), BF16),
            pltpu.VMEM((TP, REQ, LANES), F32),
            pltpu.SemaphoreType.DMA((11,)),
            pltpu.SemaphoreType.DMA((9,)),
            pltpu.SemaphoreType.DMA((9,)),
        ],
        compiler_params=pltpu.CompilerParams(
            collective_id=0, has_side_effects=True, vmem_limit_bytes=48 << 20
        ),
    )(
        tokens,
        aux,
        lengths,
        w_query,
        w_key,
        w_value,
        w_out.T,
        w_gate.reshape(SEQ, WIDTH, FFL),
        w_up.reshape(SEQ, WIDTH, FFL),
        w_down,
        key_cache.reshape(REQ, 2 * SPAN, HD),
        value_cache.reshape(REQ, 2 * SPAN, HD),
    )
    shape = key_cache.shape
    return (hidden_out, keys.reshape(shape), values.reshape(shape))


def solution(mesh):
    placed = (
        P(None, None, "seq"),
        P("seq"),
        P("seq", "tp"),
        P("seq", "tp"),
        P("seq", "tp"),
        P("tp", "seq"),
        P(),
        P(None, ("seq", "tp")),
        P(None, ("seq", "tp")),
        P(("seq", "tp"), None),
        P(None, "seq", "tp", None),
        P(None, "seq", "tp", None),
        P(),
    )
    return jax.shard_map(
        per_device,
        mesh=mesh,
        in_specs=placed,
        out_specs=(P(None, None, "seq"), P(None, "seq", "tp", None), P(None, "seq", "tp", None)),
        check_vma=False,
    )
```

```python
import functools
import math

import jax
import jax.numpy as jnp
from jax import lax
from jax.experimental import pallas as pl
from jax.experimental.pallas import tpu as pltpu
from jax.sharding import PartitionSpec as P

D = 5120
STEPS = 4
REQ = 16
ROWS = STEPS * REQ
SEQ = 64
TP = 4
WIDTH = D // SEQ
HD = 128
QH = 8
KH = 2
SPAN = 128
FFL = 128
LANES = 128
F32 = jnp.float32
BF16 = jnp.bfloat16
MESH = pl.DeviceIdType.MESH
NEG = -1e30


def split3(v):
    hi = v.astype(BF16).astype(F32)
    rest = v - hi
    mid = rest.astype(BF16).astype(F32)
    lo = rest - mid
    return hi, mid, lo


def pack(full):
    lane = lax.broadcasted_iota(jnp.int32, (32, LANES), 1)
    wide = jnp.where(lane < 64, full[0:32], pltpu.roll(full[32:64], 64, 1))
    lane = lax.broadcasted_iota(jnp.int32, (8, LANES), 1)
    thin = jnp.zeros((8, LANES), F32)
    for g in range(8):
        part = full[8 * g : 8 * g + 8]
        shift = (16 * g - 64) % LANES
        part = pltpu.roll(part, shift, 1) if shift else part
        thin = jnp.where((lane >= 16 * g) & (lane < 16 * g + 16), part, thin)
    return wide, thin


def unpack(wide, thin):
    lane = lax.broadcasted_iota(jnp.int32, (ROWS, LANES), 1)
    left = jnp.concatenate([wide, pltpu.roll(wide, 64, 1)], axis=0)
    parts = []
    for g in range(8):
        shift = (64 - 16 * g) % LANES
        parts.append(pltpu.roll(thin, shift, 1) if shift else thin)
    right = jnp.concatenate(parts, axis=0)
    return jnp.where(lane < 64, left, jnp.where(lane < WIDTH, right, 0.0))


def kernel(
    tokens_hbm,
    again_hbm,
    fgain_hbm,
    lengths_hbm,
    wq_hbm,
    wk_hbm,
    wv_hbm,
    wo_hbm,
    wg_hbm,
    wu_hbm,
    wd_hbm,
    kc_hbm,
    vc_hbm,
    hid_ref,
    ko_hbm,
    vo_hbm,
    tokens_ref,
    again_ref,
    fgain_ref,
    lengths_ref,
    wqkv,
    wo,
    wgu,
    wd,
    wdp,
    kbuf,
    vbuf,
    xbuf,
    grow,
    tmp,
    asrc,
    adst,
    ball,
    csrc,
    cdst,
    dsrc,
    dall,
    ebuf,
    fall,
    gout,
    gin,
    gown,
    hsrc,
    hdst,
    ibuf,
    lsem,
    ssem,
    rsem,
):
    me = lax.axis_index("seq")
    mt = lax.axis_index("tp")
    core = lax.rem(me, 2)
    chip = me // 2
    twin = 2 * chip + 1 - core

    barrier = pltpu.get_barrier_semaphore()

    @pl.loop(1, SEQ)
    def _(k):
        pl.semaphore_signal(
            barrier, inc=1, device_id=(lax.rem(me + k, SEQ), mt), device_id_type=MESH
        )

    @pl.loop(1, TP)
    def _(k):
        pl.semaphore_signal(
            barrier, inc=1, device_id=(me, lax.rem(mt + k, TP)), device_id_type=MESH
        )

    qw, kw = QH * HD, KH * HD
    loads = [
        (tokens_hbm, tokens_ref),
        (again_hbm, again_ref),
        (wq_hbm, wqkv.at[:, 0:qw]),
        (wk_hbm, wqkv.at[:, qw : qw + kw]),
        (wv_hbm, wqkv.at[:, qw + kw : qw + 2 * kw]),
        (lengths_hbm, lengths_ref),
        (fgain_hbm, fgain_ref),
        (kc_hbm, kbuf),
        (vc_hbm, vbuf),
        (wd_hbm, wd),
        (wo_hbm, wo),
        (wg_hbm, wgu.at[:, 0:WIDTH, 0:FFL]),
        (wu_hbm, wgu.at[:, 0:WIDTH, FFL : 2 * FFL]),
    ]
    copies = [pltpu.make_async_copy(s, d, lsem.at[i]) for i, (s, d) in enumerate(loads)]
    for c in copies:
        c.start()

    def send(phase, source, target, device):
        pltpu.make_async_remote_copy(
            src_ref=source,
            dst_ref=target,
            send_sem=ssem.at[phase],
            recv_sem=rsem.at[phase],
            device_id=device,
            device_id_type=MESH,
        ).start()

    def seq_send(phase, source, target):
        @pl.loop(1, SEQ)
        def _(k):
            p = lax.rem(me + k, SEQ)
            send(phase, source(p), target, (p, mt))

    def tp_send(phase, source, target):
        @pl.loop(1, TP)
        def _(k):
            p = lax.rem(mt + k, TP)
            send(phase, source(p), target, (me, p))

    def arrived(phase, blocks):
        pltpu.make_async_copy(blocks, blocks, rsem.at[phase]).wait()

    def sent(phase, blocks):
        pltpu.make_async_copy(blocks, blocks, ssem.at[phase]).wait()

    xbuf[...] = jnp.zeros_like(xbuf)
    for c in copies[0:2]:
        c.wait()
    xbuf[:, 0:WIDTH] = tokens_ref[...].astype(F32).reshape(ROWS, WIDTH)
    x = xbuf[...]
    squares = jnp.sum(x * x, axis=1, keepdims=True)
    normed = (x[:, 0:WIDTH] * again_ref[...].astype(F32)).astype(BF16)
    for piece, part in enumerate(split3(squares)):
        tmp[pl.ds(12 + piece, ROWS, stride=16), :] = jnp.broadcast_to(part, (ROWS, LANES))
    tmp[pl.ds(15, ROWS, stride=16), :] = jnp.zeros((ROWS, LANES), F32)
    for c in copies[2:5]:
        c.wait()
    for j in range(0, 12, 2):
        got = jnp.dot(normed, wqkv[:, j * HD : (j + 2) * HD], preferred_element_type=F32)
        tmp[pl.ds(j, ROWS, stride=16), :] = got[:, 0:HD]
        tmp[pl.ds(j + 1, ROWS, stride=16), :] = got[:, HD : 2 * HD]
    asrc[...] = tmp[...].reshape(ROWS, 16, LANES).astype(BF16)
    pl.semaphore_wait(barrier, SEQ - 1 + TP - 1)
    seq_send(0, lambda p: asrc.at[p], adst.at[me])
    adst[me] = asrc[me]

    for c in copies[5:7]:
        c.wait()
    lane1 = lax.broadcasted_iota(jnp.int32, (1, LANES), 1)
    freqs = jnp.exp(lax.rem(lane1, HD // 2).astype(F32) * (-2.0 * math.log(100000000.0) / HD))
    position = jnp.full((1, LANES), lengths_ref[lax.rem(me, REQ)] + me // REQ, jnp.int32)
    angles = position.astype(F32) * freqs
    cosine = jnp.cos(angles)
    sine = jnp.sin(angles)
    sine = jnp.where(lane1 < HD // 2, -sine, sine)
    grow[...] = fgain_ref[...].astype(F32)
    start = me * WIDTH
    line, off = start // LANES, lax.rem(start, LANES)
    shift = lax.rem(LANES - off, LANES)
    here = pltpu.roll(jnp.broadcast_to(grow[pl.ds(line, 1), :], (8, LANES)), shift, 1)
    after = jnp.broadcast_to(grow[pl.ds(lax.rem(line + 1, D // LANES), 1), :], (8, LANES))
    after = pltpu.roll(after, shift, 1)
    lane8 = lax.broadcasted_iota(jnp.int32, (8, LANES), 1)
    own_gain = jnp.where(lane8 + off < LANES, here, after)
    own_gain = jnp.where(lane8 < WIDTH, own_gain, 0.0)[0:1]
    wgu[:, WIDTH:LANES, :] = jnp.zeros((SEQ, LANES - WIDTH, 2 * FFL), BF16)
    hdst[chip] = jnp.zeros((40, LANES), BF16)
    arrived(0, adst.at[0 : SEQ - 1])
    total = jnp.sum(adst[...].astype(F32), axis=0)
    scale_in = lax.rsqrt((total[12:13] + total[13:14] + total[14:15]) / D + 1e-05)
    scaled = total * scale_in
    turned = scaled * cosine + pltpu.roll(scaled, HD // 2, 1) * sine
    sub = lax.broadcasted_iota(jnp.int32, (16, LANES), 0)
    row = jnp.where(sub < QH + KH, turned, jnp.where(sub < QH + 2 * KH, scaled, 0.0)).astype(BF16)
    ball[core, chip] = row

    @pl.loop(1, SEQ // 2)
    def _(k):
        p = lax.rem(chip + k, SEQ // 2)
        send(1, ball.at[core, chip], ball.at[core, chip], (2 * p + core, mt))

    first = me * SPAN
    r_i = lax.broadcasted_iota(jnp.int32, (2 * SPAN, ROWS), 0)
    c_i = lax.broadcasted_iota(jnp.int32, (2 * SPAN, ROWS), 1)
    where_new = r_i // 2 - c_i // 16
    pick_k = jnp.where(c_i % 16 == QH + r_i % 2, where_new, -100000)
    pick_v = jnp.where(c_i % 16 == QH + KH + r_i % 2, where_new, -100000)
    slot_i = lax.broadcasted_iota(jnp.int32, (2 * SPAN, HD), 0) // 2
    q_i = lax.broadcasted_iota(jnp.int32, (STEPS * QH, 2 * SPAN), 0)
    p_i = lax.broadcasted_iota(jnp.int32, (STEPS * QH, 2 * SPAN), 1)
    reach = jnp.where((q_i % QH) // (QH // KH) == p_i % 2, p_i // 2 - q_i // QH, 1 << 20)
    lane = lax.broadcasted_iota(jnp.int32, (STEPS * QH, LANES), 1)
    for c in copies[7:10]:
        c.wait()
    wdp[:, :, WIDTH:LANES] = jnp.zeros((SEQ, FFL, LANES - WIDTH), BF16)

    for g in range(8):
        strip = wd[:, g * 5 * LANES : (g + 1) * 5 * LANES]
        for i in range(8):
            wdp[g * 8 + i, :, 0:WIDTH] = strip[:, i * WIDTH : (i + 1) * WIDTH]

    arrived(1, ball.at[0, 0 : SEQ // 2 - 1])
    send(2, ball.at[core], ball.at[core], (twin, mt))
    arrived(2, ball.at[0])

    together = 4

    @pl.loop(0, REQ // together)
    def _(b):
        rs = [b * together + i for i in range(together)]
        lens = [lengths_ref[r] - first for r in rs]
        news = [[ball[i % 2, t * 8 + r // 2] for t in range(STEPS)] for i, r in enumerate(rs)]
        blocks = [jnp.concatenate(n, axis=0) for n in news]
        queries = [
            jnp.concatenate([n.astype(F32)[0:QH] for n in new], axis=0).astype(BF16)
            for new in news
        ]
        hot_k = [jnp.where(pick_k == n, 1.0, 0.0).astype(BF16) for n in lens]
        fresh_k = [
            jnp.dot(h, blk, preferred_element_type=F32) for h, blk in zip(hot_k, blocks)
        ]
        written = [(slot_i >= n) & (slot_i < n + STEPS) for n in lens]
        keys = [
            jnp.where(w, f, kbuf[r].astype(F32)).astype(BF16)
            for w, f, r in zip(written, fresh_k, rs)
        ]
        scores = [
            lax.dot_general(q, k, (((1,), (1,)), ((), ())), preferred_element_type=F32)
            * (HD ** (-0.5))
            for q, k in zip(queries, keys)
        ]
        hot_v = [jnp.where(pick_v == n, 1.0, 0.0).astype(BF16) for n in lens]
        fresh_v = [
            jnp.dot(h, blk, preferred_element_type=F32) for h, blk in zip(hot_v, blocks)
        ]
        values = [
            jnp.where(w, f, vbuf[r].astype(F32)).astype(BF16)
            for w, f, r in zip(written, fresh_v, rs)
        ]
        lives = [reach <= n for n in lens]
        masked = [jnp.where(live, s, NEG) for live, s in zip(lives, scores)]
        tops = [jnp.max(m, axis=1, keepdims=True) for m in masked]
        expo = [
            jnp.where(live, jnp.exp(m - top), 0.0) for live, m, top in zip(lives, masked, tops)
        ]
        denoms = [jnp.sum(e, axis=1, keepdims=True) for e in expo]
        outs = [
            jnp.dot(e.astype(BF16), v, preferred_element_type=F32) for e, v in zip(expo, values)
        ]
        for r, k, v in zip(rs, keys, values):
            kbuf[r] = k
            vbuf[r] = v
        for r, out, top, denom in zip(rs, outs, tops, denoms):
            stats = jnp.zeros((STEPS * QH, LANES), F32)
            for i, piece in enumerate(split3(top) + split3(denom)):
                stats = jnp.where(lane == i, piece, stats)
            for t in range(STEPS):
                csrc[t * REQ + r] = jnp.concatenate(
                    [out[t * QH : (t + 1) * QH], stats[t * QH : (t + 1) * QH]], axis=0
                ).astype(BF16)

    seq_send(3, lambda p: csrc.at[p], cdst.at[me])
    cdst[me] = csrc[me]
    outs = [
        pltpu.make_async_copy(kbuf, ko_hbm, lsem.at[13]),
        pltpu.make_async_copy(vbuf, vo_hbm, lsem.at[14]),
    ]
    for c in outs:
        c.start()
    arrived(3, cdst.at[0 : SEQ - 1])
    parts = cdst[...].astype(F32)
    stats = parts[:, QH : 2 * QH, :]
    lane3 = lax.broadcasted_iota(jnp.int32, (SEQ, QH, LANES), 2)
    tops = jnp.sum(jnp.where(lane3 < 3, stats, 0.0), axis=2, keepdims=True)
    dens = jnp.sum(jnp.where((lane3 >= 3) & (lane3 < 6), stats, 0.0), axis=2, keepdims=True)
    peak = jnp.max(tops, axis=0, keepdims=True)
    factor = jnp.exp(tops - peak)
    denom = jnp.sum(factor * dens, axis=0)
    attended = (jnp.sum(parts[:, 0:QH, :] * factor, axis=0) / denom).astype(BF16)
    dsrc[...] = attended
    dall[me] = attended
    seq_send(4, lambda p: dsrc, dall.at[me])
    copies[10].wait()
    arrived(4, dall.at[0 : SEQ - 1])
    tmp[0 : ROWS * QH, :] = dall[...].astype(F32).reshape(ROWS * QH, HD)
    projected = jnp.zeros((ROWS, WIDTH), F32)
    for h in range(0, QH, 2):
        left = jnp.concatenate(
            [tmp[pl.ds(h + i, ROWS, stride=QH), :].astype(BF16) for i in range(2)], axis=1
        )
        projected += lax.dot_general(
            left,
            wo[:, h * HD : (h + 2) * HD],
            (((1,), (1,)), ((), ())),
            preferred_element_type=F32,
        )
    ebuf[mt] = jnp.zeros((ROWS, LANES), F32)
    ebuf[mt, :, 0:WIDTH] = projected
    tp_send(5, lambda p: ebuf.at[mt], ebuf.at[mt])
    arrived(5, ebuf.at[0 : TP - 1])
    mixed = xbuf[...] + (ebuf[0] + ebuf[1] + ebuf[2] + ebuf[3])
    xbuf[...] = mixed
    wide, thin = pack(mixed * own_gain)
    marks = jnp.zeros((8, LANES), F32)
    for i, piece in enumerate(split3(jnp.sum(mixed * mixed, axis=1, keepdims=True))):
        for g in range(8):
            marks = jnp.where(lane8 == 16 * g + i, piece[8 * g : 8 * g + 8], marks)
    fall[core, 0] = jnp.concatenate([wide, thin, marks], axis=0).astype(BF16)
    order = (0, 3, 1, 2)
    for g in order:

        @pl.loop(8 * g if g else 1, 8 * g + 8)
        def _(k, g=g):
            p = lax.rem(chip + k, SEQ // 2)
            send(6 + g, fall.at[core, 0], fall.at[core, k], (2 * p + core, mt))

    for c in copies[11:13]:
        c.wait()
    both = jnp.zeros((ROWS, 2 * FFL), F32)
    seen = jnp.zeros((8, LANES), F32)

    def feed(half, g, both, seen):
        for k in range(8 * g, 8 * g + 8, 2):
            lefts, rights = [], []
            for i in (k, k + 1):
                block = fall[half, i].astype(F32)
                lefts.append(unpack(block[0:32], block[32:40]).astype(BF16))
                seen += block[40:48]
                rights.append(wgu[2 * lax.rem(chip + SEQ // 2 - i, SEQ // 2) + half])
            both += jnp.dot(
                jnp.concatenate(lefts, axis=1),
                jnp.concatenate(rights, axis=0),
                preferred_element_type=F32,
            )
        return both, seen

    for g in order:
        arrived(6 + g, fall.at[0, 0 : 8 if g else 7])
        mine = fall.at[core, 8 * g : 8 * g + 8]
        send(10 + g, mine, mine, (twin, mt))
        both, seen = feed(core, g, both, seen)
    for g in order:
        arrived(10 + g, fall.at[0, 0:8])
        both, seen = feed(1 - core, g, both, seen)
    total_mid = jnp.concatenate(
        [
            jnp.sum(
                jnp.where((lane8 >= 16 * g) & (lane8 < 16 * g + 16), seen, 0.0),
                axis=1,
                keepdims=True,
            )
            for g in range(8)
        ],
        axis=0,
    )
    scale_mid = lax.rsqrt(total_mid / D + 1e-05)
    gate = both[:, 0:FFL] * scale_mid
    up = both[:, FFL : 2 * FFL] * scale_mid
    hidden = ((gate / (1.0 + jnp.exp(-gate))) * up).astype(BF16)

    def down(p, half):
        two = [wdp[2 * (p + i) + half] for i in range(2)]
        got = jnp.dot(hidden, jnp.concatenate(two, axis=1), preferred_element_type=F32)
        return [
            jnp.concatenate(pack(got[:, i * LANES : (i + 1) * LANES]), axis=0) for i in range(2)
        ]

    for q in range(4):
        for p in range(8 * q, 8 * q + 8, 2):
            for i, block in enumerate(down(p, 1 - core)):
                gout[p + i] = block.astype(BF16)
        send(14 + q, gout.at[8 * q : 8 * q + 8], gin.at[8 * q : 8 * q + 8], (twin, mt))
    for p in range(0, SEQ // 2, 2):
        for i, block in enumerate(down(p, core)):
            gown[p + i] = block
    for q in range(4):
        arrived(14 + q, gin.at[0:8])

    @pl.loop(1, SEQ // 2)
    def _(k):
        p = lax.rem(chip + k, SEQ // 2)
        hsrc[p] = (gown[p] + gin[p].astype(F32)).astype(BF16)
        send(18, hsrc.at[p], hdst.at[chip], (2 * p + core, mt))

    kept = gown[chip] + gin[chip].astype(F32)
    arrived(18, hdst.at[0 : SEQ // 2 - 1])
    ibuf[mt] = kept + jnp.sum(hdst[...].astype(F32), axis=0)
    tp_send(19, lambda p: ibuf.at[mt], ibuf.at[mt])
    arrived(19, ibuf.at[0 : TP - 1])
    tail = ibuf[0] + ibuf[1] + ibuf[2] + ibuf[3]
    final = xbuf[...] + unpack(tail[0:32], tail[32:40])
    hid_ref[...] = final.astype(BF16)[:, 0:WIDTH].reshape(STEPS, REQ, WIDTH)

    sent(0, adst.at[0 : SEQ - 1])
    sent(1, ball.at[0, 0 : SEQ // 2 - 1])
    sent(2, ball.at[0])
    sent(3, cdst.at[0 : SEQ - 1])
    sent(4, dall.at[0 : SEQ - 1])
    sent(5, ebuf.at[0 : TP - 1])
    for g in range(4):
        sent(6 + g, fall.at[0, 0 : 8 if g else 7])
        sent(10 + g, fall.at[0, 0:8])
        sent(14 + g, gin.at[0:8])
    sent(18, hdst.at[0 : SEQ // 2 - 1])
    sent(19, ibuf.at[0 : TP - 1])
    for c in outs:
        c.wait()


def per_device(
    tokens,
    attn_gain,
    w_query,
    w_key,
    w_value,
    w_out,
    ffn_gain,
    w_gate,
    w_up,
    w_down,
    key_cache,
    value_cache,
    lengths,
):
    vm = pl.BlockSpec(memory_space=pltpu.VMEM)
    hb = pl.BlockSpec(memory_space=pltpu.HBM)
    cache = jax.ShapeDtypeStruct((REQ, 2 * SPAN, HD), BF16)
    hidden_out, keys, values = pl.pallas_call(
        kernel,
        out_shape=(jax.ShapeDtypeStruct((STEPS, REQ, WIDTH), BF16), cache, cache),
        in_specs=[hb] * 13,
        out_specs=(vm, hb, hb),
        scratch_shapes=[
            pltpu.VMEM((STEPS, REQ, WIDTH), BF16),
            pltpu.VMEM((1, WIDTH), BF16),
            pltpu.VMEM((D // LANES, LANES), BF16),
            pltpu.SMEM((REQ,), jnp.int32),
            pltpu.VMEM((WIDTH, (QH + 2 * KH) * HD), BF16),
            pltpu.VMEM((WIDTH, QH * HD), BF16),
            pltpu.VMEM((SEQ, LANES, 2 * FFL), BF16),
            pltpu.VMEM((FFL, D), BF16),
            pltpu.VMEM((SEQ, FFL, LANES), BF16),
            pltpu.VMEM((REQ, 2 * SPAN, HD), BF16),
            pltpu.VMEM((REQ, 2 * SPAN, HD), BF16),
            pltpu.VMEM((ROWS, LANES), F32),
            pltpu.VMEM((D // LANES, LANES), F32),
            pltpu.VMEM((ROWS * 16, LANES), F32),
            pltpu.VMEM((SEQ, 16, LANES), BF16),
            pltpu.VMEM((SEQ, 16, LANES), BF16),
            pltpu.VMEM((2, SEQ // 2, 16, LANES), BF16),
            pltpu.VMEM((SEQ, 16, LANES), BF16),
            pltpu.VMEM((SEQ, 16, LANES), BF16),
            pltpu.VMEM((QH, HD), BF16),
            pltpu.VMEM((SEQ, QH, HD), BF16),
            pltpu.VMEM((TP, ROWS, LANES), F32),
            pltpu.VMEM((2, SEQ // 2, 48, LANES), BF16),
            pltpu.VMEM((SEQ // 2, 40, LANES), BF16),
            pltpu.VMEM((SEQ // 2, 40, LANES), BF16),
            pltpu.VMEM((SEQ // 2, 40, LANES), F32),
            pltpu.VMEM((SEQ // 2, 40, LANES), BF16),
            pltpu.VMEM((SEQ // 2, 40, LANES), BF16),
            pltpu.VMEM((TP, 40, LANES), F32),
            pltpu.SemaphoreType.DMA((15,)),
            pltpu.SemaphoreType.DMA((20,)),
            pltpu.SemaphoreType.DMA((20,)),
        ],
        compiler_params=pltpu.CompilerParams(
            collective_id=0, has_side_effects=True, vmem_limit_bytes=63 << 20
        ),
    )(
        tokens,
        attn_gain.reshape(1, WIDTH),
        ffn_gain.reshape(D // LANES, LANES),
        lengths,
        w_query,
        w_key,
        w_value,
        w_out.T,
        w_gate.reshape(SEQ, WIDTH, FFL),
        w_up.reshape(SEQ, WIDTH, FFL),
        w_down,
        key_cache.reshape(REQ, 2 * SPAN, HD),
        value_cache.reshape(REQ, 2 * SPAN, HD),
    )
    shape = key_cache.shape
    return (hidden_out, keys.reshape(shape), values.reshape(shape))


def solution(mesh):
    placed = (
        P(None, None, "seq"),
        P("seq"),
        P("seq", "tp"),
        P("seq", "tp"),
        P("seq", "tp"),
        P("tp", "seq"),
        P(),
        P(None, ("seq", "tp")),
        P(None, ("seq", "tp")),
        P(("seq", "tp"), None),
        P(None, "seq", "tp", None),
        P(None, "seq", "tp", None),
        P(),
    )
    return jax.shard_map(
        per_device,
        mesh=mesh,
        in_specs=placed,
        out_specs=(P(None, None, "seq"), P(None, "seq", "tp", None), P(None, "seq", "tp", None)),
        check_vma=False,
    )
```

```python
import functools
import math

import jax
import jax.numpy as jnp
from jax import lax
from jax.experimental import pallas as pl
from jax.experimental.pallas import tpu as pltpu
from jax.sharding import PartitionSpec as P

D = 5120
STEPS = 4
REQ = 16
ROWS = STEPS * REQ
SEQ = 64
TP = 4
WIDTH = D // SEQ
HD = 128
QH = 8
KH = 2
SPAN = 128
FFL = 128
LANES = 128
F32 = jnp.float32
BF16 = jnp.bfloat16
MESH = pl.DeviceIdType.MESH
NEG = -1e30


def split3(v):
    hi = v.astype(BF16).astype(F32)
    rest = v - hi
    mid = rest.astype(BF16).astype(F32)
    lo = rest - mid
    return hi, mid, lo


def pack(full):
    lane = lax.broadcasted_iota(jnp.int32, (32, LANES), 1)
    wide = jnp.where(lane < 64, full[0:32], pltpu.roll(full[32:64], 64, 1))
    lane = lax.broadcasted_iota(jnp.int32, (8, LANES), 1)
    thin = jnp.zeros((8, LANES), F32)
    for g in range(8):
        part = full[8 * g : 8 * g + 8]
        shift = (16 * g - 64) % LANES
        part = pltpu.roll(part, shift, 1) if shift else part
        thin = jnp.where((lane >= 16 * g) & (lane < 16 * g + 16), part, thin)
    return wide, thin


def unpack(wide, thin):
    lane = lax.broadcasted_iota(jnp.int32, (ROWS, LANES), 1)
    left = jnp.concatenate([wide, pltpu.roll(wide, 64, 1)], axis=0)
    parts = []
    for g in range(8):
        shift = (64 - 16 * g) % LANES
        parts.append(pltpu.roll(thin, shift, 1) if shift else thin)
    right = jnp.concatenate(parts, axis=0)
    return jnp.where(lane < 64, left, jnp.where(lane < WIDTH, right, 0.0))


def kernel(
    tokens_hbm,
    again_hbm,
    fgain_hbm,
    lengths_hbm,
    wq_hbm,
    wk_hbm,
    wv_hbm,
    wo_hbm,
    wg_hbm,
    wu_hbm,
    wd_hbm,
    kc_hbm,
    vc_hbm,
    hid_ref,
    ko_hbm,
    vo_hbm,
    tokens_ref,
    again_ref,
    fgain_ref,
    lengths_ref,
    wqkv,
    wo,
    wgu,
    wd,
    wdp,
    kbuf,
    vbuf,
    xbuf,
    grow,
    tmp,
    asrc,
    adst,
    ball,
    csrc,
    cdst,
    dsrc,
    dall,
    ebuf,
    fall,
    gout,
    gin,
    gown,
    hsrc,
    hdst,
    ibuf,
    lsem,
    ssem,
    rsem,
):
    me = lax.axis_index("seq")
    mt = lax.axis_index("tp")
    core = lax.rem(me, 2)
    chip = me // 2
    twin = 2 * chip + 1 - core

    barrier = pltpu.get_barrier_semaphore()

    def far_first(size, act):
        act(size // 2)

        @pl.loop(1, size // 2)
        def _(i):
            act(size // 2 + i)
            act(size // 2 - i)

    far_first(
        SEQ,
        lambda k: pl.semaphore_signal(
            barrier, inc=1, device_id=(lax.rem(me + k, SEQ), mt), device_id_type=MESH
        ),
    )

    @pl.loop(1, TP)
    def _(k):
        pl.semaphore_signal(
            barrier, inc=1, device_id=(me, lax.rem(mt + k, TP)), device_id_type=MESH
        )

    qw, kw = QH * HD, KH * HD
    loads = [
        (tokens_hbm, tokens_ref),
        (again_hbm, again_ref),
        (wq_hbm, wqkv.at[:, 0:qw]),
        (wk_hbm, wqkv.at[:, qw : qw + kw]),
        (wv_hbm, wqkv.at[:, qw + kw : qw + 2 * kw]),
        (lengths_hbm, lengths_ref),
        (fgain_hbm, fgain_ref),
        (kc_hbm, kbuf),
        (vc_hbm, vbuf),
        (wd_hbm, wd),
        (wo_hbm, wo),
        (wg_hbm, wgu.at[:, 0:WIDTH, 0:FFL]),
        (wu_hbm, wgu.at[:, 0:WIDTH, FFL : 2 * FFL]),
    ]
    copies = [pltpu.make_async_copy(s, d, lsem.at[i]) for i, (s, d) in enumerate(loads)]
    for c in copies:
        c.start()

    def send(phase, source, target, device):
        pltpu.make_async_remote_copy(
            src_ref=source,
            dst_ref=target,
            send_sem=ssem.at[phase],
            recv_sem=rsem.at[phase],
            device_id=device,
            device_id_type=MESH,
        ).start()

    def seq_send(phase, source, target):
        def act(k):
            p = lax.rem(me + k, SEQ)
            send(phase, source(p), target, (p, mt))

        far_first(SEQ, act)

    def tp_send(phase, source, target):
        @pl.loop(1, TP)
        def _(k):
            p = lax.rem(mt + k, TP)
            send(phase, source(p), target, (me, p))

    def arrived(phase, blocks):
        pltpu.make_async_copy(blocks, blocks, rsem.at[phase]).wait()

    def sent(phase, blocks):
        pltpu.make_async_copy(blocks, blocks, ssem.at[phase]).wait()

    xbuf[...] = jnp.zeros_like(xbuf)
    for c in copies[0:2]:
        c.wait()
    xbuf[:, 0:WIDTH] = tokens_ref[...].astype(F32).reshape(ROWS, WIDTH)
    x = xbuf[...]
    squares = jnp.sum(x * x, axis=1, keepdims=True)
    normed = (x[:, 0:WIDTH] * again_ref[...].astype(F32)).astype(BF16)
    for piece, part in enumerate(split3(squares)):
        tmp[pl.ds(12 + piece, ROWS, stride=16), :] = jnp.broadcast_to(part, (ROWS, LANES))
    tmp[pl.ds(15, ROWS, stride=16), :] = jnp.zeros((ROWS, LANES), F32)
    for c in copies[2:5]:
        c.wait()
    for j in range(0, 12, 2):
        got = jnp.dot(normed, wqkv[:, j * HD : (j + 2) * HD], preferred_element_type=F32)
        tmp[pl.ds(j, ROWS, stride=16), :] = got[:, 0:HD]
        tmp[pl.ds(j + 1, ROWS, stride=16), :] = got[:, HD : 2 * HD]
    asrc[...] = tmp[...].reshape(ROWS, 16, LANES).astype(BF16)
    for c in copies[5:7]:
        c.wait()
    lane1 = lax.broadcasted_iota(jnp.int32, (1, LANES), 1)
    freqs = jnp.exp(lax.rem(lane1, HD // 2).astype(F32) * (-2.0 * math.log(100000000.0) / HD))
    position = jnp.full((1, LANES), lengths_ref[lax.rem(me, REQ)] + me // REQ, jnp.int32)
    angles = position.astype(F32) * freqs
    cosine = jnp.cos(angles)
    sine = jnp.sin(angles)
    sine = jnp.where(lane1 < HD // 2, -sine, sine)
    grow[...] = fgain_ref[...].astype(F32)
    start = me * WIDTH
    line, off = start // LANES, lax.rem(start, LANES)
    shift = lax.rem(LANES - off, LANES)
    here = pltpu.roll(jnp.broadcast_to(grow[pl.ds(line, 1), :], (8, LANES)), shift, 1)
    after = jnp.broadcast_to(grow[pl.ds(lax.rem(line + 1, D // LANES), 1), :], (8, LANES))
    after = pltpu.roll(after, shift, 1)
    lane8 = lax.broadcasted_iota(jnp.int32, (8, LANES), 1)
    own_gain = jnp.where(lane8 + off < LANES, here, after)
    own_gain = jnp.where(lane8 < WIDTH, own_gain, 0.0)[0:1]
    wgu[:, WIDTH:LANES, :] = jnp.zeros((SEQ, LANES - WIDTH, 2 * FFL), BF16)
    hdst[chip] = jnp.zeros((40, LANES), BF16)
    first = me * SPAN
    r_i = lax.broadcasted_iota(jnp.int32, (2 * SPAN, ROWS), 0)
    c_i = lax.broadcasted_iota(jnp.int32, (2 * SPAN, ROWS), 1)
    where_new = r_i // 2 - c_i // 16
    pick_k = jnp.where(c_i % 16 == QH + r_i % 2, where_new, -100000)
    pick_v = jnp.where(c_i % 16 == QH + KH + r_i % 2, where_new, -100000)
    slot_i = lax.broadcasted_iota(jnp.int32, (2 * SPAN, HD), 0) // 2
    q_i = lax.broadcasted_iota(jnp.int32, (STEPS * QH, 2 * SPAN), 0)
    p_i = lax.broadcasted_iota(jnp.int32, (STEPS * QH, 2 * SPAN), 1)
    reach = jnp.where((q_i % QH) // (QH // KH) == p_i % 2, p_i // 2 - q_i // QH, 1 << 20)
    lane = lax.broadcasted_iota(jnp.int32, (STEPS * QH, LANES), 1)
    for c in copies[7:10]:
        c.wait()
    wdp[:, :, WIDTH:LANES] = jnp.zeros((SEQ, FFL, LANES - WIDTH), BF16)

    for g in range(8):
        strip = wd[:, g * 5 * LANES : (g + 1) * 5 * LANES]
        for i in range(8):
            wdp[g * 8 + i, :, 0:WIDTH] = strip[:, i * WIDTH : (i + 1) * WIDTH]

    pl.semaphore_wait(barrier, SEQ - 1 + TP - 1)
    seq_send(0, lambda p: asrc.at[p], adst.at[me])
    adst[me] = asrc[me]

    arrived(0, adst.at[0 : SEQ - 1])
    total = jnp.sum(adst[...].astype(F32), axis=0)
    scale_in = lax.rsqrt((total[12:13] + total[13:14] + total[14:15]) / D + 1e-05)
    scaled = total * scale_in
    turned = scaled * cosine + pltpu.roll(scaled, HD // 2, 1) * sine
    sub = lax.broadcasted_iota(jnp.int32, (16, LANES), 0)
    row = jnp.where(sub < QH + KH, turned, jnp.where(sub < QH + 2 * KH, scaled, 0.0)).astype(BF16)
    ball[core, 0] = row
    order = (0, 3, 1, 2)
    for g in (2, 1, 3, 0):

        @pl.loop(8 * g if g else 1, 8 * g + 8)
        def _(k, g=g):
            p = lax.rem(chip + k, SEQ // 2)
            send(20 + g, ball.at[core, 0], ball.at[core, k], (2 * p + core, mt))

    for g in order:
        arrived(20 + g, ball.at[0, 0 : 8 if g else 7])
        mine = ball.at[core, 8 * g : 8 * g + 8]
        send(1, mine, mine, (twin, mt))
    arrived(1, ball.at[0])

    together = 4

    @pl.loop(0, REQ // together)
    def _(b):
        rs = [b * together + i for i in range(together)]
        lens = [lengths_ref[r] - first for r in rs]
        news = [
            [
                ball[i % 2, lax.rem(chip + SEQ // 2 - t * 8 - r // 2, SEQ // 2)]
                for t in range(STEPS)
            ]
            for i, r in enumerate(rs)
        ]
        blocks = [jnp.concatenate(n, axis=0) for n in news]
        queries = [
            jnp.concatenate([n.astype(F32)[0:QH] for n in new], axis=0).astype(BF16)
            for new in news
        ]
        hot_k = [jnp.where(pick_k == n, 1.0, 0.0).astype(BF16) for n in lens]
        fresh_k = [
            jnp.dot(h, blk, preferred_element_type=F32) for h, blk in zip(hot_k, blocks)
        ]
        written = [(slot_i >= n) & (slot_i < n + STEPS) for n in lens]
        keys = [
            jnp.where(w, f, kbuf[r].astype(F32)).astype(BF16)
            for w, f, r in zip(written, fresh_k, rs)
        ]
        scores = [
            lax.dot_general(q, k, (((1,), (1,)), ((), ())), preferred_element_type=F32)
            * (HD ** (-0.5))
            for q, k in zip(queries, keys)
        ]
        hot_v = [jnp.where(pick_v == n, 1.0, 0.0).astype(BF16) for n in lens]
        fresh_v = [
            jnp.dot(h, blk, preferred_element_type=F32) for h, blk in zip(hot_v, blocks)
        ]
        values = [
            jnp.where(w, f, vbuf[r].astype(F32)).astype(BF16)
            for w, f, r in zip(written, fresh_v, rs)
        ]
        lives = [reach <= n for n in lens]
        masked = [jnp.where(live, s, NEG) for live, s in zip(lives, scores)]
        tops = [jnp.max(m, axis=1, keepdims=True) for m in masked]
        expo = [
            jnp.where(live, jnp.exp(m - top), 0.0) for live, m, top in zip(lives, masked, tops)
        ]
        denoms = [jnp.sum(e, axis=1, keepdims=True) for e in expo]
        outs = [
            jnp.dot(e.astype(BF16), v, preferred_element_type=F32) for e, v in zip(expo, values)
        ]
        for r, k, v in zip(rs, keys, values):
            kbuf[r] = k
            vbuf[r] = v
        for r, out, top, denom in zip(rs, outs, tops, denoms):
            stats = jnp.zeros((STEPS * QH, LANES), F32)
            for i, piece in enumerate(split3(top) + split3(denom)):
                stats = jnp.where(lane == i, piece, stats)
            for t in range(STEPS):
                csrc[t * REQ + r] = jnp.concatenate(
                    [out[t * QH : (t + 1) * QH], stats[t * QH : (t + 1) * QH]], axis=0
                ).astype(BF16)

    seq_send(3, lambda p: csrc.at[p], cdst.at[me])
    cdst[me] = csrc[me]
    outs = [
        pltpu.make_async_copy(kbuf, ko_hbm, lsem.at[13]),
        pltpu.make_async_copy(vbuf, vo_hbm, lsem.at[14]),
    ]
    for c in outs:
        c.start()
    arrived(3, cdst.at[0 : SEQ - 1])
    parts = cdst[...].astype(F32)
    stats = parts[:, QH : 2 * QH, :]
    lane3 = lax.broadcasted_iota(jnp.int32, (SEQ, QH, LANES), 2)
    tops = jnp.sum(jnp.where(lane3 < 3, stats, 0.0), axis=2, keepdims=True)
    dens = jnp.sum(jnp.where((lane3 >= 3) & (lane3 < 6), stats, 0.0), axis=2, keepdims=True)
    peak = jnp.max(tops, axis=0, keepdims=True)
    factor = jnp.exp(tops - peak)
    denom = jnp.sum(factor * dens, axis=0)
    attended = (jnp.sum(parts[:, 0:QH, :] * factor, axis=0) / denom).astype(BF16)
    dsrc[...] = attended
    dall[me] = attended
    seq_send(4, lambda p: dsrc, dall.at[me])
    copies[10].wait()
    arrived(4, dall.at[0 : SEQ - 1])
    tmp[0 : ROWS * QH, :] = dall[...].astype(F32).reshape(ROWS * QH, HD)
    projected = jnp.zeros((ROWS, WIDTH), F32)
    for h in range(0, QH, 2):
        left = jnp.concatenate(
            [tmp[pl.ds(h + i, ROWS, stride=QH), :].astype(BF16) for i in range(2)], axis=1
        )
        projected += lax.dot_general(
            left,
            wo[:, h * HD : (h + 2) * HD],
            (((1,), (1,)), ((), ())),
            preferred_element_type=F32,
        )
    ebuf[mt] = jnp.zeros((ROWS, LANES), F32)
    ebuf[mt, :, 0:WIDTH] = projected
    tp_send(5, lambda p: ebuf.at[mt], ebuf.at[mt])
    arrived(5, ebuf.at[0 : TP - 1])
    mixed = xbuf[...] + (ebuf[0] + ebuf[1] + ebuf[2] + ebuf[3])
    xbuf[...] = mixed
    wide, thin = pack(mixed * own_gain)
    marks = jnp.zeros((8, LANES), F32)
    for i, piece in enumerate(split3(jnp.sum(mixed * mixed, axis=1, keepdims=True))):
        for g in range(8):
            marks = jnp.where(lane8 == 16 * g + i, piece[8 * g : 8 * g + 8], marks)
    fall[core, 0] = jnp.concatenate([wide, thin, marks], axis=0).astype(BF16)
    for g in order:

        @pl.loop(8 * g if g else 1, 8 * g + 8)
        def _(k, g=g):
            p = lax.rem(chip + k, SEQ // 2)
            send(6 + g, fall.at[core, 0], fall.at[core, k], (2 * p + core, mt))

    for c in copies[11:13]:
        c.wait()
    both = jnp.zeros((ROWS, 2 * FFL), F32)
    seen = jnp.zeros((8, LANES), F32)

    def feed(half, g, both, seen):
        for k in range(8 * g, 8 * g + 8, 2):
            lefts, rights = [], []
            for i in (k, k + 1):
                block = fall[half, i].astype(F32)
                lefts.append(unpack(block[0:32], block[32:40]).astype(BF16))
                seen += block[40:48]
                rights.append(wgu[2 * lax.rem(chip + SEQ // 2 - i, SEQ // 2) + half])
            both += jnp.dot(
                jnp.concatenate(lefts, axis=1),
                jnp.concatenate(rights, axis=0),
                preferred_element_type=F32,
            )
        return both, seen

    for g in order:
        arrived(6 + g, fall.at[0, 0 : 8 if g else 7])
        mine = fall.at[core, 8 * g : 8 * g + 8]
        send(10 + g, mine, mine, (twin, mt))
        both, seen = feed(core, g, both, seen)
    for g in order:
        arrived(10 + g, fall.at[0, 0:8])
        both, seen = feed(1 - core, g, both, seen)
    total_mid = jnp.concatenate(
        [
            jnp.sum(
                jnp.where((lane8 >= 16 * g) & (lane8 < 16 * g + 16), seen, 0.0),
                axis=1,
                keepdims=True,
            )
            for g in range(8)
        ],
        axis=0,
    )
    scale_mid = lax.rsqrt(total_mid / D + 1e-05)
    gate = both[:, 0:FFL] * scale_mid
    up = both[:, FFL : 2 * FFL] * scale_mid
    hidden = ((gate / (1.0 + jnp.exp(-gate))) * up).astype(BF16)

    def down(p, half):
        two = [wdp[2 * (p + i) + half] for i in range(2)]
        got = jnp.dot(hidden, jnp.concatenate(two, axis=1), preferred_element_type=F32)
        return [
            jnp.concatenate(pack(got[:, i * LANES : (i + 1) * LANES]), axis=0) for i in range(2)
        ]

    for q in range(4):
        for p in range(8 * q, 8 * q + 8, 2):
            for i, block in enumerate(down(p, 1 - core)):
                gout[p + i] = block.astype(BF16)
        send(14 + q, gout.at[8 * q : 8 * q + 8], gin.at[8 * q : 8 * q + 8], (twin, mt))
    for p in range(0, SEQ // 2, 2):
        for i, block in enumerate(down(p, core)):
            gown[p + i] = block
    for q in range(4):
        arrived(14 + q, gin.at[0:8])

    def pass_on(k):
        p = lax.rem(chip + k, SEQ // 2)
        hsrc[p] = (gown[p] + gin[p].astype(F32)).astype(BF16)
        send(18, hsrc.at[p], hdst.at[chip], (2 * p + core, mt))

    far_first(SEQ // 2, pass_on)

    kept = gown[chip] + gin[chip].astype(F32)
    arrived(18, hdst.at[0 : SEQ // 2 - 1])
    ibuf[mt] = kept + jnp.sum(hdst[...].astype(F32), axis=0)
    tp_send(19, lambda p: ibuf.at[mt], ibuf.at[mt])
    arrived(19, ibuf.at[0 : TP - 1])
    tail = ibuf[0] + ibuf[1] + ibuf[2] + ibuf[3]
    final = xbuf[...] + unpack(tail[0:32], tail[32:40])
    hid_ref[...] = final.astype(BF16)[:, 0:WIDTH].reshape(STEPS, REQ, WIDTH)

    sent(0, adst.at[0 : SEQ - 1])
    sent(1, ball.at[0])
    sent(3, cdst.at[0 : SEQ - 1])
    sent(4, dall.at[0 : SEQ - 1])
    sent(5, ebuf.at[0 : TP - 1])
    for g in range(4):
        sent(6 + g, fall.at[0, 0 : 8 if g else 7])
        sent(10 + g, fall.at[0, 0:8])
        sent(14 + g, gin.at[0:8])
        sent(20 + g, ball.at[0, 0 : 8 if g else 7])
    sent(18, hdst.at[0 : SEQ // 2 - 1])
    sent(19, ibuf.at[0 : TP - 1])
    for c in outs:
        c.wait()


def write_out(hid_ref, k_ref, v_ref, hid_out, k_out, v_out, kbuf, vbuf, load_sem, store_sem):
    first = pltpu.make_async_copy(hid_ref, hid_out, store_sem.at[0])
    first.start()
    loads, stores = [], [first]
    for i in range(8):
        rows = pl.ds(2 * i, 2)
        for j, (src, buf, dst) in enumerate(((k_ref, kbuf, k_out), (v_ref, vbuf, v_out))):
            load = pltpu.make_async_copy(src.at[rows], buf.at[rows], load_sem.at[2 * i + j])
            load.start()
            loads.append(load)
            stores.append(
                pltpu.make_async_copy(buf.at[rows], dst.at[rows], store_sem.at[1 + 2 * i + j])
            )
    for load, store in zip(loads, stores[1:]):
        load.wait()
        store.start()
    for store in stores:
        store.wait()


def per_device(
    tokens,
    attn_gain,
    w_query,
    w_key,
    w_value,
    w_out,
    ffn_gain,
    w_gate,
    w_up,
    w_down,
    key_cache,
    value_cache,
    lengths,
):
    vm = pl.BlockSpec(memory_space=pltpu.VMEM)
    hb = pl.BlockSpec(memory_space=pltpu.HBM)
    cache = jax.ShapeDtypeStruct((REQ, 2 * SPAN, HD), BF16)
    hidden_out, keys, values = pl.pallas_call(
        kernel,
        out_shape=(jax.ShapeDtypeStruct((STEPS, REQ, WIDTH), BF16), cache, cache),
        in_specs=[hb] * 13,
        out_specs=(vm, hb, hb),
        scratch_shapes=[
            pltpu.VMEM((STEPS, REQ, WIDTH), BF16),
            pltpu.VMEM((1, WIDTH), BF16),
            pltpu.VMEM((D // LANES, LANES), BF16),
            pltpu.SMEM((REQ,), jnp.int32),
            pltpu.VMEM((WIDTH, (QH + 2 * KH) * HD), BF16),
            pltpu.VMEM((WIDTH, QH * HD), BF16),
            pltpu.VMEM((SEQ, LANES, 2 * FFL), BF16),
            pltpu.VMEM((FFL, D), BF16),
            pltpu.VMEM((SEQ, FFL, LANES), BF16),
            pltpu.VMEM((REQ, 2 * SPAN, HD), BF16),
            pltpu.VMEM((REQ, 2 * SPAN, HD), BF16),
            pltpu.VMEM((ROWS, LANES), F32),
            pltpu.VMEM((D // LANES, LANES), F32),
            pltpu.VMEM((ROWS * 16, LANES), F32),
            pltpu.VMEM((SEQ, 16, LANES), BF16),
            pltpu.VMEM((SEQ, 16, LANES), BF16),
            pltpu.VMEM((2, SEQ // 2, 16, LANES), BF16),
            pltpu.VMEM((SEQ, 16, LANES), BF16),
            pltpu.VMEM((SEQ, 16, LANES), BF16),
            pltpu.VMEM((QH, HD), BF16),
            pltpu.VMEM((SEQ, QH, HD), BF16),
            pltpu.VMEM((TP, ROWS, LANES), F32),
            pltpu.VMEM((2, SEQ // 2, 48, LANES), BF16),
            pltpu.VMEM((SEQ // 2, 40, LANES), BF16),
            pltpu.VMEM((SEQ // 2, 40, LANES), BF16),
            pltpu.VMEM((SEQ // 2, 40, LANES), F32),
            pltpu.VMEM((SEQ // 2, 40, LANES), BF16),
            pltpu.VMEM((SEQ // 2, 40, LANES), BF16),
            pltpu.VMEM((TP, 40, LANES), F32),
            pltpu.SemaphoreType.DMA((15,)),
            pltpu.SemaphoreType.DMA((24,)),
            pltpu.SemaphoreType.DMA((24,)),
        ],
        compiler_params=pltpu.CompilerParams(
            collective_id=0, has_side_effects=True, vmem_limit_bytes=63 << 20
        ),
    )(
        tokens,
        attn_gain.reshape(1, WIDTH),
        ffn_gain.reshape(D // LANES, LANES),
        lengths,
        w_query,
        w_key,
        w_value,
        w_out.T,
        w_gate.reshape(SEQ, WIDTH, FFL),
        w_up.reshape(SEQ, WIDTH, FFL),
        w_down,
        key_cache.reshape(REQ, 2 * SPAN, HD),
        value_cache.reshape(REQ, 2 * SPAN, HD),
    )
    hidden_out, keys, values = pl.pallas_call(
        write_out,
        out_shape=(jax.ShapeDtypeStruct((STEPS, REQ, WIDTH), BF16), cache, cache),
        in_specs=[vm, hb, hb],
        out_specs=(hb, hb, hb),
        scratch_shapes=[
            pltpu.VMEM((REQ, 2 * SPAN, HD), BF16),
            pltpu.VMEM((REQ, 2 * SPAN, HD), BF16),
            pltpu.SemaphoreType.DMA((16,)),
            pltpu.SemaphoreType.DMA((17,)),
        ],
    )(hidden_out, keys, values)
    shape = key_cache.shape
    return (hidden_out, keys.reshape(shape), values.reshape(shape))


def solution(mesh):
    placed = (
        P(None, None, "seq"),
        P("seq"),
        P("seq", "tp"),
        P("seq", "tp"),
        P("seq", "tp"),
        P("tp", "seq"),
        P(),
        P(None, ("seq", "tp")),
        P(None, ("seq", "tp")),
        P(("seq", "tp"), None),
        P(None, "seq", "tp", None),
        P(None, "seq", "tp", None),
        P(),
    )
    return jax.shard_map(
        per_device,
        mesh=mesh,
        in_specs=placed,
        out_specs=(P(None, None, "seq"), P(None, "seq", "tp", None), P(None, "seq", "tp", None)),
        check_vma=False,
    )
```

```python
import functools
import math

import jax
import jax.numpy as jnp
from jax import lax
from jax.experimental import pallas as pl
from jax.experimental.pallas import tpu as pltpu
from jax.sharding import PartitionSpec as P

D = 5120
STEPS = 4
REQ = 16
ROWS = STEPS * REQ
SEQ = 64
TP = 4
WIDTH = D // SEQ
HD = 128
QH = 8
KH = 2
SPAN = 128
FFL = 128
LANES = 128
F32 = jnp.float32
BF16 = jnp.bfloat16
MESH = pl.DeviceIdType.MESH
NEG = -1e30


def split3(v):
    hi = v.astype(BF16).astype(F32)
    rest = v - hi
    mid = rest.astype(BF16).astype(F32)
    lo = rest - mid
    return hi, mid, lo


def pack(full):
    lane = lax.broadcasted_iota(jnp.int32, (32, LANES), 1)
    wide = jnp.where(lane < 64, full[0:32], pltpu.roll(full[32:64], 64, 1))
    lane = lax.broadcasted_iota(jnp.int32, (8, LANES), 1)
    thin = jnp.zeros((8, LANES), F32)
    for g in range(8):
        part = full[8 * g : 8 * g + 8]
        shift = (16 * g - 64) % LANES
        part = pltpu.roll(part, shift, 1) if shift else part
        thin = jnp.where((lane >= 16 * g) & (lane < 16 * g + 16), part, thin)
    return wide, thin


def unpack(wide, thin):
    lane = lax.broadcasted_iota(jnp.int32, (ROWS, LANES), 1)
    left = jnp.concatenate([wide, pltpu.roll(wide, 64, 1)], axis=0)
    parts = []
    for g in range(8):
        shift = (64 - 16 * g) % LANES
        parts.append(pltpu.roll(thin, shift, 1) if shift else thin)
    right = jnp.concatenate(parts, axis=0)
    return jnp.where(lane < 64, left, jnp.where(lane < WIDTH, right, 0.0))


def kernel(
    tokens_hbm,
    again_hbm,
    fgain_hbm,
    lengths_hbm,
    wq_hbm,
    wk_hbm,
    wv_hbm,
    wo_hbm,
    wg_hbm,
    wu_hbm,
    wd_hbm,
    kc_hbm,
    vc_hbm,
    hid_ref,
    ko_hbm,
    vo_hbm,
    tokens_ref,
    again_ref,
    fgain_ref,
    lengths_ref,
    wqkv,
    wo,
    wgu,
    wd,
    wdp,
    kbuf,
    vbuf,
    xbuf,
    grow,
    tmp,
    asrc,
    adst,
    ball,
    csrc,
    cdst,
    dsrc,
    dall,
    ebuf,
    fall,
    gout,
    gin,
    gown,
    hsrc,
    hdst,
    ibuf,
    lsem,
    ssem,
    rsem,
):
    me = lax.axis_index("seq")
    mt = lax.axis_index("tp")
    core = lax.rem(me, 2)
    chip = me // 2
    twin = 2 * chip + 1 - core

    barrier = pltpu.get_barrier_semaphore()

    def far_first(size, act):
        act(size // 2)

        @pl.loop(1, size // 2)
        def _(i):
            act(size // 2 + i)
            act(size // 2 - i)

    far_first(
        SEQ,
        lambda k: pl.semaphore_signal(
            barrier, inc=1, device_id=(lax.rem(me + k, SEQ), mt), device_id_type=MESH
        ),
    )

    @pl.loop(1, TP)
    def _(k):
        pl.semaphore_signal(
            barrier, inc=1, device_id=(me, lax.rem(mt + k, TP)), device_id_type=MESH
        )

    qw, kw = QH * HD, KH * HD
    loads = [
        (tokens_hbm, tokens_ref),
        (again_hbm, again_ref),
        (wq_hbm, wqkv.at[:, 0:qw]),
        (wk_hbm, wqkv.at[:, qw : qw + kw]),
        (wv_hbm, wqkv.at[:, qw + kw : qw + 2 * kw]),
        (lengths_hbm, lengths_ref),
        (fgain_hbm, fgain_ref),
        (kc_hbm, kbuf),
        (vc_hbm, vbuf),
        (wd_hbm, wd),
        (wo_hbm, wo),
        (wg_hbm, wgu.at[:, 0:WIDTH, 0:FFL]),
        (wu_hbm, wgu.at[:, 0:WIDTH, FFL : 2 * FFL]),
    ]
    copies = [pltpu.make_async_copy(s, d, lsem.at[i]) for i, (s, d) in enumerate(loads)]
    for c in copies:
        c.start()

    def send(phase, source, target, device):
        pltpu.make_async_remote_copy(
            src_ref=source,
            dst_ref=target,
            send_sem=ssem.at[phase],
            recv_sem=rsem.at[phase],
            device_id=device,
            device_id_type=MESH,
        ).start()

    def seq_send(phase, source, target):
        def act(k):
            p = lax.rem(me + k, SEQ)
            send(phase, source(p), target, (p, mt))

        far_first(SEQ, act)

    def tp_send(phase, source, target):
        @pl.loop(1, TP)
        def _(k):
            p = lax.rem(mt + k, TP)
            send(phase, source(p), target, (me, p))

    def arrived(phase, blocks):
        pltpu.make_async_copy(blocks, blocks, rsem.at[phase]).wait()

    def sent(phase, blocks):
        pltpu.make_async_copy(blocks, blocks, ssem.at[phase]).wait()

    xbuf[...] = jnp.zeros_like(xbuf)
    for c in copies[0:2]:
        c.wait()
    xbuf[:, 0:WIDTH] = tokens_ref[...].astype(F32).reshape(ROWS, WIDTH)
    x = xbuf[...]
    squares = jnp.sum(x * x, axis=1, keepdims=True)
    normed = (x[:, 0:WIDTH] * again_ref[...].astype(F32)).astype(BF16)
    for piece, part in enumerate(split3(squares)):
        tmp[pl.ds(12 + piece, ROWS, stride=16), :] = jnp.broadcast_to(part, (ROWS, LANES))
    tmp[pl.ds(15, ROWS, stride=16), :] = jnp.zeros((ROWS, LANES), F32)
    for c in copies[2:5]:
        c.wait()
    for j in range(0, 12, 2):
        got = jnp.dot(normed, wqkv[:, j * HD : (j + 2) * HD], preferred_element_type=F32)
        tmp[pl.ds(j, ROWS, stride=16), :] = got[:, 0:HD]
        tmp[pl.ds(j + 1, ROWS, stride=16), :] = got[:, HD : 2 * HD]
    asrc[...] = tmp[...].reshape(ROWS, 16, LANES).astype(BF16)
    for c in copies[5:7]:
        c.wait()
    lane1 = lax.broadcasted_iota(jnp.int32, (1, LANES), 1)
    freqs = jnp.exp(lax.rem(lane1, HD // 2).astype(F32) * (-2.0 * math.log(100000000.0) / HD))
    position = jnp.full((1, LANES), lengths_ref[lax.rem(me, REQ)] + me // REQ, jnp.int32)
    angles = position.astype(F32) * freqs
    cosine = jnp.cos(angles)
    sine = jnp.sin(angles)
    sine = jnp.where(lane1 < HD // 2, -sine, sine)
    grow[...] = fgain_ref[...].astype(F32)
    start = me * WIDTH
    line, off = start // LANES, lax.rem(start, LANES)
    shift = lax.rem(LANES - off, LANES)
    here = pltpu.roll(jnp.broadcast_to(grow[pl.ds(line, 1), :], (8, LANES)), shift, 1)
    after = jnp.broadcast_to(grow[pl.ds(lax.rem(line + 1, D // LANES), 1), :], (8, LANES))
    after = pltpu.roll(after, shift, 1)
    lane8 = lax.broadcasted_iota(jnp.int32, (8, LANES), 1)
    own_gain = jnp.where(lane8 + off < LANES, here, after)
    own_gain = jnp.where(lane8 < WIDTH, own_gain, 0.0)[0:1]
    wgu[:, WIDTH:LANES, :] = jnp.zeros((SEQ, LANES - WIDTH, 2 * FFL), BF16)
    hdst[chip] = jnp.zeros((40, LANES), BF16)
    first = me * SPAN
    r_i = lax.broadcasted_iota(jnp.int32, (2 * SPAN, ROWS), 0)
    c_i = lax.broadcasted_iota(jnp.int32, (2 * SPAN, ROWS), 1)
    where_new = r_i // 2 - c_i // 16
    pick_k = jnp.where(c_i % 16 == QH + r_i % 2, where_new, -100000)
    pick_v = jnp.where(c_i % 16 == QH + KH + r_i % 2, where_new, -100000)
    slot_i = lax.broadcasted_iota(jnp.int32, (2 * SPAN, HD), 0) // 2
    q_i = lax.broadcasted_iota(jnp.int32, (STEPS * QH, 2 * SPAN), 0)
    p_i = lax.broadcasted_iota(jnp.int32, (STEPS * QH, 2 * SPAN), 1)
    reach = jnp.where((q_i % QH) // (QH // KH) == p_i % 2, p_i // 2 - q_i // QH, 1 << 20)
    lane = lax.broadcasted_iota(jnp.int32, (STEPS * QH, LANES), 1)
    for c in copies[7:10]:
        c.wait()
    wdp[:, :, WIDTH:LANES] = jnp.zeros((SEQ, FFL, LANES - WIDTH), BF16)

    for g in range(8):
        strip = wd[:, g * 5 * LANES : (g + 1) * 5 * LANES]
        for i in range(8):
            wdp[g * 8 + i, :, 0:WIDTH] = strip[:, i * WIDTH : (i + 1) * WIDTH]

    pl.semaphore_wait(barrier, SEQ - 1 + TP - 1)
    seq_send(0, lambda p: asrc.at[p], adst.at[me])
    adst[me] = asrc[me]

    arrived(0, adst.at[0 : SEQ - 1])
    total = jnp.sum(adst[...].astype(F32), axis=0)
    scale_in = lax.rsqrt((total[12:13] + total[13:14] + total[14:15]) / D + 1e-05)
    scaled = total * scale_in
    turned = scaled * cosine + pltpu.roll(scaled, HD // 2, 1) * sine
    sub = lax.broadcasted_iota(jnp.int32, (16, LANES), 0)
    row = jnp.where(sub < QH + KH, turned, jnp.where(sub < QH + 2 * KH, scaled, 0.0)).astype(BF16)
    ball[core, 0] = row
    order = (0, 3, 1, 2)
    for g in (2, 1, 3, 0):

        @pl.loop(8 * g if g else 1, 8 * g + 8)
        def _(k, g=g):
            p = lax.rem(chip + k, SEQ // 2)
            send(20 + g, ball.at[core, 0], ball.at[core, k], (2 * p + core, mt))

    for g in order:
        arrived(20 + g, ball.at[0, 0 : 8 if g else 7])
        mine = ball.at[core, 8 * g : 8 * g + 8]
        send(1, mine, mine, (twin, mt))
    arrived(1, ball.at[0])

    together = 4

    @pl.loop(0, REQ // together)
    def _(b):
        rs = [b * together + i for i in range(together)]
        lens = [lengths_ref[r] - first for r in rs]
        news = [
            [
                ball[i % 2, lax.rem(chip + SEQ // 2 - t * 8 - r // 2, SEQ // 2)]
                for t in range(STEPS)
            ]
            for i, r in enumerate(rs)
        ]
        blocks = [jnp.concatenate(n, axis=0) for n in news]
        queries = [
            jnp.concatenate([n.astype(F32)[0:QH] for n in new], axis=0).astype(BF16)
            for new in news
        ]
        hot_k = [jnp.where(pick_k == n, 1.0, 0.0).astype(BF16) for n in lens]
        fresh_k = [
            jnp.dot(h, blk, preferred_element_type=F32) for h, blk in zip(hot_k, blocks)
        ]
        written = [(slot_i >= n) & (slot_i < n + STEPS) for n in lens]
        keys = [
            jnp.where(w, f, kbuf[r].astype(F32)).astype(BF16)
            for w, f, r in zip(written, fresh_k, rs)
        ]
        scores = [
            lax.dot_general(q, k, (((1,), (1,)), ((), ())), preferred_element_type=F32)
            * (HD ** (-0.5))
            for q, k in zip(queries, keys)
        ]
        hot_v = [jnp.where(pick_v == n, 1.0, 0.0).astype(BF16) for n in lens]
        fresh_v = [
            jnp.dot(h, blk, preferred_element_type=F32) for h, blk in zip(hot_v, blocks)
        ]
        values = [
            jnp.where(w, f, vbuf[r].astype(F32)).astype(BF16)
            for w, f, r in zip(written, fresh_v, rs)
        ]
        lives = [reach <= n for n in lens]
        masked = [jnp.where(live, s, NEG) for live, s in zip(lives, scores)]
        tops = [jnp.max(m, axis=1, keepdims=True) for m in masked]
        expo = [
            jnp.where(live, jnp.exp(m - top), 0.0) for live, m, top in zip(lives, masked, tops)
        ]
        denoms = [jnp.sum(e, axis=1, keepdims=True) for e in expo]
        outs = [
            jnp.dot(e.astype(BF16), v, preferred_element_type=F32) for e, v in zip(expo, values)
        ]
        for r, k, v in zip(rs, keys, values):
            kbuf[r] = k
            vbuf[r] = v
        for r, out, top, denom in zip(rs, outs, tops, denoms):
            stats = jnp.zeros((STEPS * QH, LANES), F32)
            for i, piece in enumerate(split3(top) + split3(denom)):
                stats = jnp.where(lane == i, piece, stats)
            for t in range(STEPS):
                csrc[t * REQ + r] = jnp.concatenate(
                    [out[t * QH : (t + 1) * QH], stats[t * QH : (t + 1) * QH]], axis=0
                ).astype(BF16)

    seq_send(3, lambda p: csrc.at[p], cdst.at[me])
    cdst[me] = csrc[me]
    outs = [
        pltpu.make_async_copy(kbuf, ko_hbm, lsem.at[13]),
        pltpu.make_async_copy(vbuf, vo_hbm, lsem.at[14]),
    ]
    for c in outs:
        c.start()
    arrived(3, cdst.at[0 : SEQ - 1])
    parts = cdst[...].astype(F32)
    stats = parts[:, QH : 2 * QH, :]
    lane3 = lax.broadcasted_iota(jnp.int32, (SEQ, QH, LANES), 2)
    tops = jnp.sum(jnp.where(lane3 < 3, stats, 0.0), axis=2, keepdims=True)
    dens = jnp.sum(jnp.where((lane3 >= 3) & (lane3 < 6), stats, 0.0), axis=2, keepdims=True)
    peak = jnp.max(tops, axis=0, keepdims=True)
    factor = jnp.exp(tops - peak)
    denom = jnp.sum(factor * dens, axis=0)
    attended = (jnp.sum(parts[:, 0:QH, :] * factor, axis=0) / denom).astype(BF16)
    dsrc[...] = attended
    dall[me] = attended
    seq_send(4, lambda p: dsrc, dall.at[me])
    copies[10].wait()
    arrived(4, dall.at[0 : SEQ - 1])
    tmp[0 : ROWS * QH, :] = dall[...].astype(F32).reshape(ROWS * QH, HD)
    projected = jnp.zeros((ROWS, WIDTH), F32)
    for h in range(0, QH, 2):
        left = jnp.concatenate(
            [tmp[pl.ds(h + i, ROWS, stride=QH), :].astype(BF16) for i in range(2)], axis=1
        )
        projected += lax.dot_general(
            left,
            wo[:, h * HD : (h + 2) * HD],
            (((1,), (1,)), ((), ())),
            preferred_element_type=F32,
        )
    ebuf[mt] = jnp.zeros((ROWS, LANES), F32)
    ebuf[mt, :, 0:WIDTH] = projected
    tp_send(5, lambda p: ebuf.at[mt], ebuf.at[mt])
    arrived(5, ebuf.at[0 : TP - 1])
    mixed = xbuf[...] + (ebuf[0] + ebuf[1] + ebuf[2] + ebuf[3])
    xbuf[...] = mixed
    wide, thin = pack(mixed * own_gain)
    marks = jnp.zeros((8, LANES), F32)
    for i, piece in enumerate(split3(jnp.sum(mixed * mixed, axis=1, keepdims=True))):
        for g in range(8):
            marks = jnp.where(lane8 == 16 * g + i, piece[8 * g : 8 * g + 8], marks)
    fall[core, 0] = jnp.concatenate([wide, thin, marks], axis=0).astype(BF16)
    for g in order:

        @pl.loop(8 * g if g else 1, 8 * g + 8)
        def _(k, g=g):
            p = lax.rem(chip + k, SEQ // 2)
            send(6 + g, fall.at[core, 0], fall.at[core, k], (2 * p + core, mt))

    for c in copies[11:13]:
        c.wait()
    both = jnp.zeros((ROWS, 2 * FFL), F32)
    seen = jnp.zeros((8, LANES), F32)

    def feed(half, g, both, seen):
        for k in range(8 * g, 8 * g + 8, 2):
            lefts, rights = [], []
            for i in (k, k + 1):
                block = fall[half, i].astype(F32)
                lefts.append(unpack(block[0:32], block[32:40]).astype(BF16))
                seen += block[40:48]
                rights.append(wgu[2 * lax.rem(chip + SEQ // 2 - i, SEQ // 2) + half])
            both += jnp.dot(
                jnp.concatenate(lefts, axis=1),
                jnp.concatenate(rights, axis=0),
                preferred_element_type=F32,
            )
        return both, seen

    for g in order:
        arrived(6 + g, fall.at[0, 0 : 8 if g else 7])
        mine = fall.at[core, 8 * g : 8 * g + 8]
        send(10 + g, mine, mine, (twin, mt))
        both, seen = feed(core, g, both, seen)
    for g in order:
        arrived(10 + g, fall.at[0, 0:8])
        both, seen = feed(1 - core, g, both, seen)
    total_mid = jnp.concatenate(
        [
            jnp.sum(
                jnp.where((lane8 >= 16 * g) & (lane8 < 16 * g + 16), seen, 0.0),
                axis=1,
                keepdims=True,
            )
            for g in range(8)
        ],
        axis=0,
    )
    scale_mid = lax.rsqrt(total_mid / D + 1e-05)
    gate = both[:, 0:FFL] * scale_mid
    up = both[:, FFL : 2 * FFL] * scale_mid
    hidden = ((gate / (1.0 + jnp.exp(-gate))) * up).astype(BF16)

    def down(p, half):
        two = [wdp[2 * (p + i) + half] for i in range(2)]
        got = jnp.dot(hidden, jnp.concatenate(two, axis=1), preferred_element_type=F32)
        return [
            jnp.concatenate(pack(got[:, i * LANES : (i + 1) * LANES]), axis=0) for i in range(2)
        ]

    for q in range(4):
        for p in range(8 * q, 8 * q + 8, 2):
            for i, block in enumerate(down(p, 1 - core)):
                gout[p + i] = block.astype(BF16)
        send(14 + q, gout.at[8 * q : 8 * q + 8], gin.at[8 * q : 8 * q + 8], (twin, mt))
    for p in range(0, SEQ // 2, 2):
        for i, block in enumerate(down(p, core)):
            gown[p + i] = block
    for q in range(4):
        arrived(14 + q, gin.at[0:8])

    def pass_on(k):
        p = lax.rem(chip + k, SEQ // 2)
        hsrc[p] = (gown[p] + gin[p].astype(F32)).astype(BF16)
        send(18, hsrc.at[p], hdst.at[chip], (2 * p + core, mt))

    far_first(SEQ // 2, pass_on)

    kept = gown[chip] + gin[chip].astype(F32)
    arrived(18, hdst.at[0 : SEQ // 2 - 1])
    ibuf[mt] = kept + jnp.sum(hdst[...].astype(F32), axis=0)
    tp_send(19, lambda p: ibuf.at[mt], ibuf.at[mt])
    arrived(19, ibuf.at[0 : TP - 1])
    tail = ibuf[0] + ibuf[1] + ibuf[2] + ibuf[3]
    final = xbuf[...] + unpack(tail[0:32], tail[32:40])
    hid_ref[...] = final.astype(BF16)[:, 0:WIDTH].reshape(STEPS, REQ, WIDTH)

    sent(0, adst.at[0 : SEQ - 1])
    sent(1, ball.at[0])
    sent(3, cdst.at[0 : SEQ - 1])
    sent(4, dall.at[0 : SEQ - 1])
    sent(5, ebuf.at[0 : TP - 1])
    for g in range(4):
        sent(6 + g, fall.at[0, 0 : 8 if g else 7])
        sent(10 + g, fall.at[0, 0:8])
        sent(14 + g, gin.at[0:8])
        sent(20 + g, ball.at[0, 0 : 8 if g else 7])
    sent(18, hdst.at[0 : SEQ // 2 - 1])
    sent(19, ibuf.at[0 : TP - 1])
    for c in outs:
        c.wait()


def write_out(
    hid_ref, k_ref, v_ref, hid_out, k_out, v_out, hbuf, kbuf, vbuf, load_sem, store_sem
):
    moves = []
    for i in range(8):
        rows = pl.ds(2 * i, 2)
        for src, buf, dst in ((k_ref, kbuf, k_out), (v_ref, vbuf, v_out)):
            moves.append((src.at[rows], buf.at[rows], dst.at[rows]))
    moves.append((hid_ref, hbuf, hid_out))
    loads = [pltpu.make_async_copy(m[0], m[1], load_sem.at[i]) for i, m in enumerate(moves)]
    stores = [pltpu.make_async_copy(m[1], m[2], store_sem.at[i]) for i, m in enumerate(moves)]
    for load in loads:
        load.start()
    for load, store in zip(loads, stores):
        load.wait()
        store.start()
    for store in stores:
        store.wait()


def per_device(
    tokens,
    attn_gain,
    w_query,
    w_key,
    w_value,
    w_out,
    ffn_gain,
    w_gate,
    w_up,
    w_down,
    key_cache,
    value_cache,
    lengths,
):
    vm = pl.BlockSpec(memory_space=pltpu.VMEM)
    hb = pl.BlockSpec(memory_space=pltpu.HBM)
    cache = jax.ShapeDtypeStruct((REQ, 2 * SPAN, HD), BF16)
    hidden_out, keys, values = pl.pallas_call(
        kernel,
        out_shape=(jax.ShapeDtypeStruct((STEPS, REQ, WIDTH), BF16), cache, cache),
        in_specs=[hb] * 13,
        out_specs=(vm, hb, hb),
        scratch_shapes=[
            pltpu.VMEM((STEPS, REQ, WIDTH), BF16),
            pltpu.VMEM((1, WIDTH), BF16),
            pltpu.VMEM((D // LANES, LANES), BF16),
            pltpu.SMEM((REQ,), jnp.int32),
            pltpu.VMEM((WIDTH, (QH + 2 * KH) * HD), BF16),
            pltpu.VMEM((WIDTH, QH * HD), BF16),
            pltpu.VMEM((SEQ, LANES, 2 * FFL), BF16),
            pltpu.VMEM((FFL, D), BF16),
            pltpu.VMEM((SEQ, FFL, LANES), BF16),
            pltpu.VMEM((REQ, 2 * SPAN, HD), BF16),
            pltpu.VMEM((REQ, 2 * SPAN, HD), BF16),
            pltpu.VMEM((ROWS, LANES), F32),
            pltpu.VMEM((D // LANES, LANES), F32),
            pltpu.VMEM((ROWS * 16, LANES), F32),
            pltpu.VMEM((SEQ, 16, LANES), BF16),
            pltpu.VMEM((SEQ, 16, LANES), BF16),
            pltpu.VMEM((2, SEQ // 2, 16, LANES), BF16),
            pltpu.VMEM((SEQ, 16, LANES), BF16),
            pltpu.VMEM((SEQ, 16, LANES), BF16),
            pltpu.VMEM((QH, HD), BF16),
            pltpu.VMEM((SEQ, QH, HD), BF16),
            pltpu.VMEM((TP, ROWS, LANES), F32),
            pltpu.VMEM((2, SEQ // 2, 48, LANES), BF16),
            pltpu.VMEM((SEQ // 2, 40, LANES), BF16),
            pltpu.VMEM((SEQ // 2, 40, LANES), BF16),
            pltpu.VMEM((SEQ // 2, 40, LANES), F32),
            pltpu.VMEM((SEQ // 2, 40, LANES), BF16),
            pltpu.VMEM((SEQ // 2, 40, LANES), BF16),
            pltpu.VMEM((TP, 40, LANES), F32),
            pltpu.SemaphoreType.DMA((15,)),
            pltpu.SemaphoreType.DMA((24,)),
            pltpu.SemaphoreType.DMA((24,)),
        ],
        compiler_params=pltpu.CompilerParams(
            collective_id=0, has_side_effects=True, vmem_limit_bytes=63 << 20
        ),
    )(
        tokens,
        attn_gain.reshape(1, WIDTH),
        ffn_gain.reshape(D // LANES, LANES),
        lengths,
        w_query,
        w_key,
        w_value,
        w_out.T,
        w_gate.reshape(SEQ, WIDTH, FFL),
        w_up.reshape(SEQ, WIDTH, FFL),
        w_down,
        key_cache.reshape(REQ, 2 * SPAN, HD),
        value_cache.reshape(REQ, 2 * SPAN, HD),
    )
    hidden_out, keys, values = pl.pallas_call(
        write_out,
        out_shape=(jax.ShapeDtypeStruct((STEPS, REQ, WIDTH), BF16), cache, cache),
        in_specs=[hb, hb, hb],
        out_specs=(hb, hb, hb),
        scratch_shapes=[
            pltpu.VMEM((STEPS, REQ, WIDTH), BF16),
            pltpu.VMEM((REQ, 2 * SPAN, HD), BF16),
            pltpu.VMEM((REQ, 2 * SPAN, HD), BF16),
            pltpu.SemaphoreType.DMA((17,)),
            pltpu.SemaphoreType.DMA((17,)),
        ],
    )(hidden_out, keys, values)
    shape = key_cache.shape
    return (hidden_out, keys.reshape(shape), values.reshape(shape))


def solution(mesh):
    placed = (
        P(None, None, "seq"),
        P("seq"),
        P("seq", "tp"),
        P("seq", "tp"),
        P("seq", "tp"),
        P("tp", "seq"),
        P(),
        P(None, ("seq", "tp")),
        P(None, ("seq", "tp")),
        P(("seq", "tp"), None),
        P(None, "seq", "tp", None),
        P(None, "seq", "tp", None),
        P(),
    )
    return jax.shard_map(
        per_device,
        mesh=mesh,
        in_specs=placed,
        out_specs=(P(None, None, "seq"), P(None, "seq", "tp", None), P(None, "seq", "tp", None)),
        check_vma=False,
    )
```
